32 devices in a mesh: seq: 4 (over x, core), exp: 8 (over z, y).
Axes of the slice: x: 2, y: 2, z: 4, core: 2. Of those that a mesh axis runs over, the one named last changes fastest.
Arguments:
- residual_in: bfloat16 [4096, 2048], P(('seq', 'exp')), may hold values from -8 to 8
- ssm_input: bfloat16 [4096, 2048], P(('seq', 'exp')), may hold values from -6 to 6
- ssm_b: bfloat16 [4096, 128], P(('seq', 'exp')), may hold values from -6 to 6
- ssm_c: bfloat16 [4096, 128], P(('seq', 'exp')), may hold values from -0.5 to 0.5
- log_decay: float32 [4096, 32], P(('seq', 'exp')), may hold values from -2 to 0, as said below
- skip_gain: float32 [32], replicated, may hold values from 0.5 to 1.5
- out_proj: bfloat16 [2048, 2048], replicated, may hold values from -0.125 to 0.125
- norm_gain: float32 [2048], replicated, may hold values from 0.5 to 1.5
- router: bfloat16 [2048, 16], replicated, may hold values from -1 to 1
- assignment: int32 [4096, 1], P(('seq', 'exp')), may hold values from 0 to 15; in each aligned block of 128 rows (0 to 127, 128 to 255, ...) at most 16 rows name the same one
- expert_gate: bfloat16 [32, 2048, 704], P(('seq', 'exp')), may hold values from -0.125 to 0.125
- expert_up: bfloat16 [32, 2048, 704], P(('seq', 'exp')), may hold values from -0.125 to 0.125
- expert_down: bfloat16 [32, 704, 2048], P(('seq', 'exp')), may hold values from -0.15625 to 0.15625
Outputs:
- layer_out: bfloat16 [4096, 2048], P(('seq', 'exp'))
- route_weight: float32 [4096], P(('seq', 'exp'))
The draws below stay inside these ranges and needn't reach their ends.
Inputs may be any that keep to these rules, and one draw needn't show every extreme that they name: `log_decay`: every entry is negative. `assignment`: on the rows of one device no expert is named more than 16 times; in every draw some expert is named exactly 16 times on some device.
All inputs are finite; a program needn't handle non-finite values.
Results may differ from the reference program's by a relative error of at most 0.009.
Values may be sent and summed in bfloat16 or wider, within the bound.
A program may use at most 576 MiB of HBM per device.

```python
import math
import jax
import jax.numpy as jnp
import numpy as np
from jax import lax

D = 2048
MIXER_HEADS = 32
HEAD_DIM = 64
STATE = 128
FF = 1408
BLOCK = 128
SINK_ITERS = 8
TOK_DEV = 128
EXPERTS = 16
CAPACITY = 16
SEQUENCE_TOKENS = 4096
N_SEQ = 4
N_EXP = 8


def draw_log_decay(key, part):
    random_subkeys = jax.random.split(key, 7)
    slow_count = max(1, MIXER_HEADS // 2)
    head_order = jax.random.permutation(random_subkeys[0], MIXER_HEADS)
    slow_heads = head_order < slow_count
    slow_rate = jnp.exp(jax.random.uniform(random_subkeys[1], (MIXER_HEADS,), jnp.float32, -2.5, -0.5)) / SEQUENCE_TOKENS
    fast_rate = jnp.exp(jax.random.uniform(random_subkeys[2], (MIXER_HEADS,), jnp.float32, -0.25, 0.25)) / 40.0
    head_decay_rate = jnp.where(slow_heads, slow_rate, fast_rate)
    token_factor = jnp.exp(jax.random.uniform(random_subkeys[3], (SEQUENCE_TOKENS // TOK_DEV, TOK_DEV, MIXER_HEADS), jnp.float32, -0.7, 0.7))
    block_factor = jnp.exp(jax.random.uniform(random_subkeys[4], (SEQUENCE_TOKENS // TOK_DEV, 1, MIXER_HEADS), jnp.float32, -0.35, 0.35))
    scale_multiplier = (token_factor * block_factor).reshape(SEQUENCE_TOKENS, MIXER_HEADS)
    spike_location = jax.random.randint(random_subkeys[5], (2,), 0, SEQUENCE_TOKENS)
    spike_depth = jax.random.uniform(random_subkeys[6], (2, MIXER_HEADS), jnp.float32, 0.2, 0.5)
    token_positions = jnp.arange(SEQUENCE_TOKENS)
    spike_start_token = (token_positions[:, None] == spike_location[0]).astype(jnp.float32) * (-jnp.log(1.0 - spike_depth[0]))[None, :]
    spike_second_token = (token_positions[:, None] == spike_location[1]).astype(jnp.float32) * (-jnp.log(1.0 - spike_depth[1]))[None, :]
    return -(head_decay_rate[None, :] * scale_multiplier) - spike_start_token - spike_second_token


def cluster_sides(key):
    base_key = jax.random.fold_in(key, 7919)
    random_subkeys = jax.random.split(base_key, 3)
    direction = jnp.where(jax.random.bernoulli(random_subkeys[0], 0.5, (D,)), 1.0, -1.0).astype(jnp.float32)
    share_start = 0.3
    share_end = 0.86
    placing = jnp.arange(SEQUENCE_TOKENS).astype(jnp.float32) / SEQUENCE_TOKENS
    share = share_start + (share_end - share_start) * placing
    token_side = jnp.where(jax.random.bernoulli(random_subkeys[1], share), 1.0, -1.0).astype(jnp.float32)
    expert_side = jnp.where(jax.random.permutation(random_subkeys[2], EXPERTS) < EXPERTS // 2, 1.0, -1.0).astype(jnp.float32)
    return (direction, token_side, expert_side)


def draw_residual_in(key, part):
    direction, token_side, expert_side = cluster_sides(key)
    spread_key = jax.random.fold_in(key, 104729)
    random_part = jax.random.truncated_normal(spread_key, -6.0, 6.0, (SEQUENCE_TOKENS, D), jnp.float32)
    strength = 1.0
    return (random_part + strength * token_side[:, None] * direction[None, :]).astype(jnp.bfloat16)


def draw_router(key, part):
    direction, token_side, expert_side = cluster_sides(key)
    spread_key = jax.random.fold_in(key, 15485863)
    random_part = jax.random.truncated_normal(spread_key, -6.0, 6.0, (D, EXPERTS), jnp.float32)
    return (random_part * D ** (-0.5) + 4.5 / D * direction[:, None] * expert_side[None, :]).astype(jnp.bfloat16)


def levels(stream_key, dims, cuts, least, top_value):
    gain = 1.0
    for dim, blocks in cuts:
        heights = jax.random.uniform(jax.random.fold_in(jax.random.fold_in(stream_key, 6), dim), (blocks,), jnp.float32, least / len(cuts), top_value / len(cuts))
        gain = gain * jnp.repeat(jnp.exp(heights), dims[dim] // blocks).reshape((-1,) + (1,) * (len(dims) - 1 - dim))
    return gain


def assign_block(rng, own, number, rows, count, top, most, lean):
    sequence = jax.random.permutation(rng, count)
    crowded, ordinary = portions_of(count, rows * top, most, lean, True), portions_of(count, rows * top, most, lean, False)
    places = jnp.arange(count)

    def named(lengths, turn):
        used = int((lengths > 0).sum())
        fixed = max(1, used // 4)
        passed = fixed + (places - fixed + turn * (used - fixed)) % max(1, count - fixed)
        return jnp.zeros((count,), jnp.int32).at[sequence[jnp.where(places < fixed, places, passed)]].set(jnp.asarray(lengths, jnp.int32))

    lengths = jnp.where(number % 4 == 0, named(crowded, number // 4), named(ordinary, number - number // 4 - 1))
    mixed = jax.random.permutation(jax.random.fold_in(own, 3), count)
    giver, sink = mixed[0:count // 2 * 2:2], mixed[1:count // 2 * 2:2]
    room = jnp.minimum(lengths[giver] - 1, most - lengths[sink]) // 2
    room = jnp.where((giver == sequence[0]) | (sink == sequence[0]) | (lengths[sink] == 0), 0, jnp.maximum(room, 0))
    passed = jax.random.randint(jax.random.fold_in(own, 4), (count // 2,), 0, 1 << 20) % (room + 1)
    lengths = lengths.at[giver].add(-passed).at[sink].add(passed)
    labels = jnp.searchsorted(jnp.cumsum(lengths), jnp.arange(rows * top), side="right").astype(jnp.int32)
    grid = labels.reshape(top, rows).T
    grid = grid[jax.random.permutation(jax.random.fold_in(own, 1), rows)]
    turn = jax.random.randint(jax.random.fold_in(own, 2), (rows, 1), 0, top)
    return jnp.take_along_axis(grid, (jnp.arange(top)[None, :] + turn) % top, axis=1)


def portions_of(amount, total, bound, slope, full):
    weights = [(1 << 20) // math.isqrt(rank ** slope) + 1 for rank in range(1, amount + 1)]
    largest = bound if full else min(bound, max(-(-total // amount), total * weights[0] // sum(weights)))
    least = 1 if total - largest >= amount - 1 else 0
    given, spare = [largest] + [least] * (amount - 1), total - largest - least * (amount - 1)
    while spare > 0:
        movable = [i for i in range(1, amount) if given[i] < largest] or [i for i in range(1, amount) if given[i] < bound]
        mass, remaining = sum([weights[i] for i in movable]), spare
        for i in movable:
            more = min(bound - given[i], max(1, remaining * weights[i] // mass), spare)
            given[i] = given[i] + more
            spare = spare - more
    return np.array(given)


def centred(key, shape, scale, bound, cuts=(), kind=jnp.bfloat16):
    array = jax.random.normal(key, shape, jnp.float32) * scale
    if len(cuts) > 0:
        array = levels(key, shape, cuts, -0.22, 0.18) * array
    return jnp.clip(array, min=-bound, max=bound).astype(kind)


def setup_inputs(seed: int = 0) -> dict:
    seeds = jax.random.split(jax.random.key(seed), 14)
    residual_in = draw_residual_in(jax.random.fold_in(seeds[13], 71), 0)
    ssm_input = centred(seeds[1], (SEQUENCE_TOKENS, MIXER_HEADS * HEAD_DIM), 1.0, 6.0, ((0, 32),))
    ssm_b = centred(seeds[2], (SEQUENCE_TOKENS, STATE), 1.0, 6.0, ((0, 32),))
    ssm_c = centred(seeds[3], (SEQUENCE_TOKENS, STATE), STATE ** -0.5, 0.5, ((0, 32),))
    log_decay = draw_log_decay(jax.random.fold_in(seeds[13], 71), 0)
    skip_gain = jnp.clip(jax.random.uniform(seeds[5], (MIXER_HEADS,), jnp.float32, 0.5, 1.5), 0.5, 1.5)
    out_proj = centred(seeds[6], (MIXER_HEADS * HEAD_DIM, D), (MIXER_HEADS * HEAD_DIM) ** -0.5, 0.125)
    norm_gain = jnp.clip(1.0 + 0.1 * jax.random.normal(seeds[7], (D,), jnp.float32), 0.5, 1.5)
    router = draw_router(jax.random.fold_in(seeds[13], 71), 0)
    assignment_keys = jax.random.split(jax.random.fold_in(seeds[9], 1), SEQUENCE_TOKENS // TOK_DEV)
    assignment_turns = jax.random.permutation(jax.random.fold_in(seeds[9], 3), SEQUENCE_TOKENS // TOK_DEV)
    assignment = jax.vmap(lambda own, number: assign_block(jax.random.fold_in(seeds[9], 2), own, number, TOK_DEV, EXPERTS, 1, CAPACITY, 2))(assignment_keys, assignment_turns).reshape((SEQUENCE_TOKENS, 1))
    expert_gate = centred(seeds[10], (2 * EXPERTS, D, FF // 2), D ** -0.5, 0.125, ((0, 32),))
    expert_up = centred(seeds[11], (2 * EXPERTS, D, FF // 2), D ** -0.5, 0.125, ((0, 32),))
    expert_down = centred(seeds[12], (2 * EXPERTS, FF // 2, D), FF ** -0.5, 0.15625, ((0, 32),))
    return {"residual_in": residual_in, "ssm_input": ssm_input, "ssm_b": ssm_b, "ssm_c": ssm_c, "log_decay": log_decay, "skip_gain": skip_gain, "out_proj": out_proj, "norm_gain": norm_gain, "router": router, "assignment": assignment, "expert_gate": expert_gate, "expert_up": expert_up, "expert_down": expert_down}


def block_terms(values, b_matrix, c_matrix, decay):
    length = values.shape[0]
    values_float = values.astype(jnp.float32)
    cumulative = jnp.cumsum(decay, axis=0)
    weight = jnp.sqrt(-jnp.expm1(2.0 * decay))
    scores = jnp.dot(c_matrix, b_matrix.T, preferred_element_type=jnp.float32)
    leading = cumulative.T
    distance = leading[:, :, None] - leading[:, None, :]
    causal = jnp.arange(length)[:, None] >= jnp.arange(length)[None, :]
    decay_mix = jnp.where(causal[None, :, :], jnp.exp(jnp.minimum(distance, 0.0)), 0.0) * (weight.T[:, None, :] * scores[None, :, :])
    decay_mix = lax.optimization_barrier(decay_mix.astype(jnp.bfloat16))
    inner_part = jnp.einsum('hts,shp->thp', decay_mix.astype(jnp.float32), values_float, precision=lax.Precision.HIGHEST)
    tail_weight = jnp.exp(cumulative[-1][None, :] - cumulative) * weight
    tail_in = lax.optimization_barrier((values_float * tail_weight[:, :, None]).astype(jnp.bfloat16))
    block_state = jnp.einsum('sn,shp->hnp', b_matrix.astype(jnp.float32), tail_in.astype(jnp.float32), precision=lax.Precision.HIGHEST)
    return (inner_part, cumulative, block_state)

def reference(residual_in, ssm_input, ssm_b, ssm_c, log_decay, skip_gain, out_proj, norm_gain, router, assignment, expert_gate, expert_up, expert_down):
    head_count = skip_gain.shape[0]
    total_rows, row_width = ssm_input.shape
    head_size = row_width // head_count
    block_count = total_rows // BLOCK
    values = ssm_input.reshape(block_count, BLOCK, head_count, head_size)
    b_blocks = ssm_b.reshape(block_count, BLOCK, STATE)
    c_blocks = ssm_c.reshape(block_count, BLOCK, STATE)
    d_blocks = log_decay.reshape(block_count, BLOCK, head_count)

    def advance(entry, pieces):
        block_values, b_matrix, c_matrix, decay = pieces
        inner_part, cumulative, block_state = block_terms(block_values, b_matrix, c_matrix, decay)
        entry_rounded = lax.optimization_barrier(entry.astype(jnp.bfloat16))
        carried = jnp.exp(cumulative)[:, :, None] * jnp.einsum('tn,hnp->thp', c_matrix.astype(jnp.float32), entry_rounded.astype(jnp.float32), precision=lax.Precision.HIGHEST)
        updated = jnp.exp(cumulative[-1])[:, None, None] * entry + block_state
        return (updated, inner_part + carried)
    initial = jnp.zeros((head_count, STATE, head_size), jnp.float32)
    final_state, outputs = lax.scan(advance, initial, (values, b_blocks, c_blocks, d_blocks))
    scan_out = (outputs + skip_gain[None, None, :, None] * values.astype(jnp.float32)).reshape(total_rows, row_width).astype(jnp.bfloat16)
    mixed = residual_in.astype(jnp.float32) + jnp.dot(scan_out, out_proj, preferred_element_type=jnp.float32)
    scale = lax.rsqrt(lax.optimization_barrier(jnp.mean(mixed * mixed, axis=1, keepdims=True)) + 1e-05)
    normed = (mixed * scale * norm_gain[None, :]).astype(jnp.bfloat16)
    kernel = jnp.exp(jnp.dot(normed, router, preferred_element_type=jnp.float32))
    column = jnp.ones((EXPERTS,), jnp.float32)
    for sweep in range(SINK_ITERS):
        row_scale = 1.0 / lax.optimization_barrier(jnp.sum(kernel * column[None, :], axis=1))
        column = 1.0 / lax.optimization_barrier(jnp.sum(kernel * row_scale[:, None], axis=0))
    chosen = assignment[:, 0].astype(jnp.int32)
    chosen_hot = chosen[:, None] == jnp.arange(EXPERTS).astype(jnp.int32)[None, :]
    weighted = kernel * column[None, :]
    route_weight = EXPERTS * lax.optimization_barrier(jnp.sum(jnp.where(chosen_hot, weighted, 0.0), axis=1)) / lax.optimization_barrier(jnp.sum(weighted, axis=1))
    device_count = N_SEQ * N_EXP
    hot_int = chosen_hot.astype(jnp.int32).reshape(device_count, TOK_DEV, EXPERTS)
    slot = lax.optimization_barrier(jnp.sum(jnp.cumsum(hot_int, axis=1) * hot_int, axis=2)) - 1
    device_ids = jnp.arange(device_count).astype(jnp.int32)[:, None]
    position = (chosen.reshape(device_count, TOK_DEV) * (device_count * CAPACITY) + device_ids * CAPACITY + slot).reshape(total_rows).astype(jnp.int32)
    buffer = jnp.zeros((EXPERTS * device_count * CAPACITY, D), jnp.bfloat16).at[position].set(normed)
    buffer = buffer.reshape(EXPERTS, device_count * CAPACITY, D)
    gate_pairs = expert_gate.reshape(EXPERTS, 2, D, FF // 2)
    up_pairs = expert_up.reshape(EXPERTS, 2, D, FF // 2)
    down_pairs = expert_down.reshape(EXPERTS, 2, FF // 2, D)

    def run_expert(pieces):
        rows_in, gate_pair, up_pair, down_pair = pieces
        gate_full = jnp.concatenate([gate_pair[0], gate_pair[1]], axis=1)
        up_full = jnp.concatenate([up_pair[0], up_pair[1]], axis=1)
        down_full = jnp.concatenate([down_pair[0], down_pair[1]], axis=0)
        gate_val = jnp.dot(rows_in, gate_full, preferred_element_type=jnp.float32)
        up_val = jnp.dot(rows_in, up_full, preferred_element_type=jnp.float32)
        hidden = (jax.nn.silu(gate_val) * up_val).astype(jnp.bfloat16)
        return jnp.dot(hidden, down_full, preferred_element_type=jnp.float32).astype(jnp.bfloat16)
    results = lax.map(run_expert, (buffer, gate_pairs, up_pairs, down_pairs)).reshape(-1, D)
    expert_out = results[position]
    layer_out = (mixed + route_weight[:, None] * expert_out.astype(jnp.float32)).astype(jnp.bfloat16)
    return (layer_out, route_weight)
```

```python
import functools

import jax
import jax.numpy as jnp
from jax import lax
from jax.experimental import pallas as pl
from jax.experimental.pallas import tpu as pltpu
from jax.sharding import PartitionSpec as P

SINK_ITERS = 8
LANES = 128
MESH = pl.DeviceIdType.MESH


def place(flat):
    across = lax.axis_size("exp")
    return (flat // across, flat % across)


def own_index():
    return lax.axis_index("seq") * lax.axis_size("exp") + lax.axis_index("exp")


def device_count():
    return lax.axis_size("seq") * lax.axis_size("exp")


def meet_all(me, devices):
    barrier = pltpu.get_barrier_semaphore()

    @pl.loop(1, devices)
    def _(step):
        pl.semaphore_signal(
            barrier, inc=1, device_id=place((me + step) % devices), device_id_type=MESH
        )

    pl.semaphore_wait(barrier, devices - 1)


def entry_kernel(pieces, src_ref, factor_ref, out_ref, arrived, totals, gathered, scanned, entered, entries,
                 factors, products, spans, go_send, go_recv, factor_send, factor_recv, up_send, up_recv,
                 span_send, span_recv, down_send, down_recv, back_send, back_recv):
    line, spot = lax.axis_index("seq"), lax.axis_index("exp")
    lines = lax.axis_size("seq")
    level, side = spot // 2, spot % 2
    mine = 2 * line + side
    near = 2 * lines
    levels = lax.axis_size("exp") // 2
    rows, cols = arrived.shape[2:]
    part = rows // levels

    def near_place(peer):
        return (peer // 2, 2 * level + peer % 2)

    def far_place(peer):
        return (line, 2 * peer + side)

    def remote(src, dst, send, recv, device):
        return pltpu.make_async_remote_copy(
            src_ref=src, dst_ref=dst, send_sem=send, recv_sem=recv, device_id=device, device_id_type=MESH)

    def region(ref, piece, slot):
        return ref.at[pl.ds(piece * rows, rows), pl.ds(pl.multiple_of(slot * cols, cols), cols)]

    def go_copy(piece, peer, slot):
        return remote(region(src_ref, piece, peer), arrived.at[piece, slot], go_send.at[piece, peer],
                      go_recv.at[piece, slot], near_place(peer))

    def factor_copy(peer, slot):
        return remote(factor_ref.at[peer], factors.at[slot], factor_send.at[peer], factor_recv.at[slot],
                      near_place(peer))

    def up_copy(piece, peer, slot):
        return remote(totals.at[piece, peer], gathered.at[piece, slot], up_send.at[piece, peer],
                      up_recv.at[piece, slot], far_place(peer))

    def span_copy(peer, slot):
        return remote(products, spans.at[slot], span_send.at[peer], span_recv.at[slot], far_place(peer))

    def down_copy(piece, peer, slot):
        return remote(scanned.at[piece, peer], entered.at[piece, slot], down_send.at[piece, peer],
                      down_recv.at[piece, slot], far_place(peer))

    def back_copy(piece, peer, slot):
        return remote(entries.at[piece, peer], region(out_ref, piece, slot), back_send.at[piece, peer],
                      back_recv.at[piece, slot], near_place(peer))

    barrier = pltpu.get_barrier_semaphore()

    @pl.loop(1, near)
    def _(step):
        pl.semaphore_signal(barrier, inc=1, device_id=near_place((mine + step) % near), device_id_type=MESH)

    @pl.loop(1, levels)
    def _(step):
        pl.semaphore_signal(barrier, inc=1, device_id=far_place((level + step) % levels), device_id_type=MESH)

    factors[mine] = factor_ref[mine]
    for piece in range(pieces):
        arrived[piece, mine] = region(src_ref, piece, mine)[...]
    pl.semaphore_wait(barrier, near + levels - 2)

    @pl.loop(1, near)
    def _(step):
        peer = (mine + step) % near
        factor_copy(peer, mine).start()
        go_copy(0, peer, mine).start()

    for piece in range(1, pieces):
        @pl.loop(1, near)
        def _(step):
            go_copy(piece, (mine + step) % near, mine).start()

    for piece in range(pieces):
        @pl.loop(1, near)
        def _(step):
            peer = (mine + near - step) % near
            if piece == 0:
                factor_copy(peer, peer).wait_recv()
            go_copy(piece, peer, peer).wait_recv()

        if piece == 0:
            @pl.loop(0, lines)
            def _(at):
                products[at] = factors[2 * at] * factors[2 * at + 1]

            spans[level] = products[...]

            @pl.loop(1, levels)
            def _(step):
                span_copy((level + step) % levels, level).start()

        @pl.loop(0, lines)
        def _(at):
            both = factors[2 * at + 1] * arrived[piece, 2 * at].astype(jnp.float32)
            both = both + arrived[piece, 2 * at + 1].astype(jnp.float32)
            totals[piece, :, at] = both.astype(totals.dtype).reshape(levels, part, cols)

        gathered[piece, level] = totals[piece, level]

        @pl.loop(1, levels)
        def _(step):
            up_copy(piece, (level + step) % levels, level).start()

    for piece in range(pieces):
        @pl.loop(1, levels)
        def _(step):
            peer = (level + levels - step) % levels
            if piece == 0:
                span_copy(peer, peer).wait_recv()
            up_copy(piece, peer, peer).wait_recv()

        def advance(k, state):
            at, floor = k // levels, k % levels
            scanned[piece, floor, at] = state.astype(scanned.dtype)
            return spans[floor, at] * state + gathered[piece, floor, at].astype(jnp.float32)

        lax.fori_loop(0, lines * levels, advance, jnp.zeros((part, cols), jnp.float32))
        entered[piece, level] = scanned[piece, level]

        @pl.loop(1, levels)
        def _(step):
            down_copy(piece, (level + step) % levels, level).start()

    for piece in range(pieces):
        @pl.loop(1, levels)
        def _(step):
            peer = (level + levels - step) % levels
            down_copy(piece, peer, peer).wait_recv()

        @pl.loop(0, lines)
        def _(at):
            first = entered[piece, :, at].reshape(rows, cols)
            entries[piece, 2 * at] = first
            second = factors[2 * at] * first.astype(jnp.float32) + arrived[piece, 2 * at].astype(jnp.float32)
            entries[piece, 2 * at + 1] = second.astype(entries.dtype)

        @pl.loop(1, near)
        def _(step):
            back_copy(piece, (mine + step) % near, mine).start()

        region(out_ref, piece, mine)[...] = entries[piece, mine]

    @pl.loop(1, near)
    def _(step):
        peer = (mine + near - step) % near
        factor_copy(peer, peer).wait_send()
        for piece in range(pieces):
            go_copy(piece, peer, peer).wait_send()
            back_copy(piece, peer, peer).wait_recv()
            back_copy(piece, peer, peer).wait_send()

    @pl.loop(1, levels)
    def _(step):
        peer = (level + levels - step) % levels
        span_copy(peer, peer).wait_send()
        for piece in range(pieces):
            up_copy(piece, peer, peer).wait_send()
            down_copy(piece, peer, peer).wait_send()


def entering(block_state, factor):
    lines, levels = lax.axis_size("seq"), lax.axis_size("exp") // 2
    near = 2 * lines
    state_size, width = block_state.shape
    pieces = max(1, min(2, state_size // (16 * levels)))
    rows, cols = state_size // pieces, width // near
    part = rows // levels
    dma = pltpu.SemaphoreType.DMA
    vmem = pl.BlockSpec(memory_space=pltpu.VMEM)
    flat = pltpu.VMEM((pieces, near, rows, cols), jnp.bfloat16)
    deep = pltpu.VMEM((pieces, levels, lines, part, cols), jnp.bfloat16)
    nears, fars = dma((pieces, near)), dma((pieces, levels))
    return pl.pallas_call(
        functools.partial(entry_kernel, pieces),
        out_shape=jax.ShapeDtypeStruct((state_size, width), jnp.bfloat16),
        in_specs=[vmem, vmem],
        out_specs=vmem,
        scratch_shapes=[
            flat, deep, deep, deep, deep, flat,
            pltpu.VMEM((near, 1, cols), jnp.float32),
            pltpu.VMEM((lines, 1, cols), jnp.float32),
            pltpu.VMEM((levels, lines, 1, cols), jnp.float32),
            nears, nears, dma((near,)), dma((near,)), fars, fars,
            dma((levels,)), dma((levels,)), fars, fars, nears, nears,
        ],
        compiler_params=pltpu.CompilerParams(
            collective_id=0, has_side_effects=True, vmem_limit_bytes=16 << 20
        ),
        name="entry_states",
    )(block_state.astype(jnp.bfloat16), factor.reshape(near, 1, cols))


def expert_kernel(devices, group, packed_ref, kernel_ref, hot_ref, gate_hbm, up_hbm, down_hbm, out_ref, weight_ref,
                  table_ref, rows, halves, partial, summed, gate, up, down, block,
                  go_send, go_recv, pass_send, pass_recv, swap_send, swap_recv, back_send, back_recv,
                  near_send, near_recv, far_send, far_recv, own_sem, weight_sem):
    line, spot = lax.axis_index("seq"), lax.axis_index("exp")
    lines, spots = lax.axis_size("seq"), lax.axis_size("exp")
    me = line * spots + spot
    side, mine = me % 2, me // 2
    experts = devices // 2
    partner = me + 1 - 2 * side
    capacity, width = packed_ref.shape[1:]
    turns = experts // group

    def remote(src, dst, send, recv, device):
        return pltpu.make_async_remote_copy(
            src_ref=src, dst_ref=dst, send_sem=send, recv_sem=recv, device_id=device, device_id_type=MESH)

    def row_copy(other, slot):
        return remote(packed_ref.at[other], rows.at[side, slot], go_send.at[other], go_recv.at[slot],
                      place(2 * other + side))

    def pass_copy(at, slot):
        return remote(rows.at[side, slot], rows.at[at, slot], pass_send.at[slot], pass_recv.at[slot],
                      place(partner))

    def swap_copy(slot):
        return remote(halves.at[1 - side, slot], partial.at[slot], swap_send.at[slot], swap_recv.at[slot],
                      place(partner))

    def back_copy(other, slot):
        return remote(summed.at[other], out_ref.at[slot], back_send.at[other], back_recv.at[slot],
                      place(2 * other + side))

    def near_copy(other, slot):
        return remote(kernel_ref, table_ref.at[line, slot], near_send.at[other], near_recv.at[slot],
                      (line, other))

    def far_copy(other, slot):
        return remote(table_ref.at[line], table_ref.at[slot], far_send.at[other], far_recv.at[slot],
                      (other, spot))

    own_rows = pltpu.make_async_copy(packed_ref.at[mine], rows.at[side, mine], own_sem.at[0])
    own_table = pltpu.make_async_copy(kernel_ref, table_ref.at[line, spot], own_sem.at[1])
    own_rows.start()
    own_table.start()
    loads = [
        pltpu.make_async_copy(gate_hbm, gate, weight_sem.at[0]),
        pltpu.make_async_copy(up_hbm, up, weight_sem.at[1]),
        pltpu.make_async_copy(down_hbm, down, weight_sem.at[2]),
    ]
    for load in loads:
        load.start()
    meet_all(me, devices)

    @pl.loop(1, experts)
    def _(step):
        row_copy((mine + step) % experts, mine).start()

    @pl.loop(1, spots)
    def _(step):
        near_copy((spot + step) % spots, spot).start()

    own_rows.wait()
    pass_copy(side, mine).start()
    for load in loads:
        load.wait()

    def source_of(turn, at):
        return (mine + 2 * experts - (turn * group + at)) % experts

    @pl.loop(0, turns + 2)
    def _(turn):
        @pl.when(turn < turns)
        def _():
            @pl.loop(0, group)
            def _(at):
                @pl.when(turn * group + at > 0)
                def _():
                    source = source_of(turn, at)
                    row_copy(source, source).wait_recv()
                    pass_copy(side, source).start()

        @pl.when((turn >= 1) & (turn <= turns))
        def _():
            @pl.loop(0, group)
            def _(at):
                pass_copy(1 - side, source_of(turn - 1, at)).wait_recv()

            sources = [source_of(turn - 1, at) for at in range(group)]
            places = [(k, source, (k * group + at) * capacity)
                      for k in range(2) for at, source in enumerate(sources)]
            for k, source, start in places:
                block[start:start + capacity] = rows[k, source]
            taken = block[...]
            across = (((1,), (1,)), ((), ()))
            gate_val = lax.dot_general(taken, gate[...], across, preferred_element_type=jnp.float32)
            up_val = lax.dot_general(taken, up[...], across, preferred_element_type=jnp.float32)
            hidden = (gate_val / (1.0 + jnp.exp(-gate_val)) * up_val).astype(jnp.bfloat16)
            piece = 512
            for column in range(0, width, piece):
                made = jnp.dot(hidden, down[:, column:column + piece], preferred_element_type=jnp.float32)
                made = made.astype(halves.dtype)
                for k, source, start in places:
                    halves[k, source, :, column:column + piece] = made[start:start + capacity]

            @pl.loop(0, group)
            def _(at):
                swap_copy(source_of(turn - 1, at)).start()

        @pl.when(turn >= 2)
        def _():
            @pl.loop(0, group)
            def _(at):
                source = source_of(turn - 2, at)
                swap_copy(source).wait_recv()
                summed[source] = (
                    halves[side, source].astype(jnp.float32) + partial[source].astype(jnp.float32)
                ).astype(summed.dtype)

                @pl.when((turn - 2) * group + at > 0)
                def _():
                    back_copy(source, mine).start()

        @pl.when(turn == 1)
        def _():
            own_table.wait()

            @pl.loop(1, spots)
            def _(step):
                near_copy((spot + step) % spots, (spot + step) % spots).wait_recv()

            @pl.loop(1, lines)
            def _(step):
                far_copy((line + step) % lines, line).start()

    own_out = pltpu.make_async_copy(summed.at[mine], out_ref.at[mine], own_sem.at[0])
    own_out.start()

    @pl.loop(1, lines)
    def _(step):
        other = (line + step) % lines
        far_copy(other, other).wait_recv()
        far_copy(other, other).wait_send()

    choices, length = kernel_ref.shape

    def sweep(_, column):
        def add(at, totals):
            part = table_ref[at]
            row_scale = 1.0 / jnp.sum(part * column[None], axis=1, keepdims=True)
            return totals + jnp.sum(part * row_scale, axis=0)

        totals = lax.fori_loop(0, lines, add, jnp.zeros((choices, length), jnp.float32))
        return 1.0 / jnp.sum(totals, axis=1, keepdims=True)

    column = lax.fori_loop(0, SINK_ITERS, sweep, jnp.ones((choices, 1), jnp.float32))
    weighted = kernel_ref[...] * column
    picked = jnp.sum(jnp.where(hot_ref[...] > 0.0, weighted, 0.0), axis=0, keepdims=True)
    weight_ref[...] = choices * picked / jnp.sum(weighted, axis=0, keepdims=True)

    @pl.loop(1, spots)
    def _(step):
        near_copy((spot + step) % spots, spot).wait_send()

    @pl.loop(0, experts)
    def _(step):
        pass_copy(side, step).wait_send()
        swap_copy(step).wait_send()

    @pl.loop(1, experts)
    def _(step):
        other = (mine + step) % experts
        row_copy(other, other).wait_send()
        back_copy(other, other).wait_recv()
        back_copy(other, other).wait_send()

    own_out.wait()


def expert_layer(packed, kernel, hot, gate_half, up_half, down_half):
    devices = device_count()
    lines, spots = lax.axis_size("seq"), lax.axis_size("exp")
    experts, capacity, width = packed.shape
    hidden_units = down_half.shape[0]
    group = 8
    dma = pltpu.SemaphoreType.DMA
    vmem = pl.BlockSpec(memory_space=pltpu.VMEM)
    anywhere = pl.BlockSpec(memory_space=pl.ANY)
    single = pltpu.VMEM((experts, capacity, width), packed.dtype)
    double = pltpu.VMEM((2, experts, capacity, width), packed.dtype)
    weights = pltpu.VMEM((hidden_units, width), packed.dtype)
    each = dma((experts,))
    return pl.pallas_call(
        functools.partial(expert_kernel, devices, group),
        out_shape=(
            jax.ShapeDtypeStruct((experts, capacity, width), packed.dtype),
            jax.ShapeDtypeStruct((1, kernel.shape[1]), kernel.dtype),
        ),
        in_specs=[vmem, vmem, vmem, anywhere, anywhere, anywhere],
        out_specs=(vmem, vmem),
        scratch_shapes=[
            pltpu.VMEM((lines, spots, *kernel.shape), kernel.dtype),
            double, double, single, single, weights, weights, weights,
            pltpu.VMEM((2 * group * capacity, width), packed.dtype),
            each, each, each, each, each, each, each, each,
            dma((spots,)), dma((spots,)), dma((lines,)), dma((lines,)), dma((2,)), dma((3,)),
        ],
        compiler_params=pltpu.CompilerParams(collective_id=1, has_side_effects=True),
        name="expert_layer",
    )(packed, kernel, hot, gate_half.T, up_half.T, down_half)


def widen(per_head, width):
    return jnp.repeat(per_head, width // per_head.shape[-1], axis=-1)


def block_terms(values, b_matrix, c_matrix, decay):
    length, head_count, head_size = values.shape
    row_width = head_count * head_size
    cumulative = jnp.cumsum(decay, axis=0)
    weight = jnp.sqrt(-jnp.expm1(2.0 * decay))
    flat_values = values.reshape(length, row_width)
    tail_weight = jnp.exp(cumulative[-1:] - cumulative) * weight
    tail_in = (flat_values.astype(jnp.float32) * widen(tail_weight, row_width)).astype(jnp.bfloat16)
    block_state = jnp.einsum("sn,sc->nc", b_matrix, tail_in, preferred_element_type=jnp.float32)
    scores = jnp.einsum("tn,sn->ts", c_matrix, b_matrix, preferred_element_type=jnp.float32)
    leading = cumulative.T
    distance = leading[:, :, None] - leading[:, None, :]
    causal = jnp.arange(length)[:, None] >= jnp.arange(length)[None, :]
    decay_mix = jnp.where(causal, jnp.exp(jnp.minimum(distance, 0.0)), 0.0) * (
        weight.T[:, None, :] * scores[None, :, :]
    )
    decay_mix = decay_mix.astype(jnp.bfloat16)
    inner_part = jnp.einsum("hts,shp->thp", decay_mix, values, preferred_element_type=jnp.float32)
    return (inner_part.reshape(length, row_width), cumulative, block_state)


def per_device(
    residual_in,
    ssm_input,
    ssm_b,
    ssm_c,
    log_decay,
    skip_gain,
    out_proj,
    norm_gain,
    router,
    assignment,
    expert_gate,
    expert_up,
    expert_down,
):
    head_count = skip_gain.shape[0]
    length, row_width = ssm_input.shape
    head_size = row_width // head_count
    model_width = residual_in.shape[1]
    values = ssm_input.reshape(length, head_count, head_size)
    inner_part, cumulative, block_state = block_terms(values, ssm_b, ssm_c, log_decay)
    entry_rounded = entering(block_state, widen(jnp.exp(cumulative[-1]), row_width))
    carried = widen(jnp.exp(cumulative), row_width) * jnp.dot(
        ssm_c, entry_rounded, preferred_element_type=jnp.float32
    )
    skip_wide = widen(skip_gain, row_width)
    scan_out = (inner_part + carried + skip_wide[None, :] * ssm_input.astype(jnp.float32)).astype(
        jnp.bfloat16
    )
    mixed = residual_in.astype(jnp.float32) + jnp.dot(
        scan_out, out_proj, preferred_element_type=jnp.float32
    )
    scale = lax.rsqrt(jnp.mean(mixed * mixed, axis=1, keepdims=True) + 1e-05)
    normed = (mixed * scale * norm_gain[None, :]).astype(jnp.bfloat16)
    kernel = jnp.exp(jnp.einsum("de,td->et", router, normed, preferred_element_type=jnp.float32))
    experts = router.shape[1]
    capacity = max(16, 2 * length // experts)
    chosen = assignment[:, 0]
    hot = (chosen[:, None] == jnp.arange(experts, dtype=jnp.int32)[None, :]).astype(jnp.float32)
    upto = (jnp.arange(length)[:, None] >= jnp.arange(length)[None, :]).astype(jnp.bfloat16)
    counts = jnp.dot(upto, hot.astype(jnp.bfloat16), preferred_element_type=jnp.float32)
    slot = jnp.sum(counts * hot, axis=1).astype(jnp.int32) - 1
    position = chosen * capacity + slot
    spread = (
        position[:, None] == jnp.arange(experts * capacity, dtype=jnp.int32)[None, :]
    ).astype(jnp.bfloat16)
    packed = jnp.einsum("ts,td->sd", spread, normed, preferred_element_type=jnp.float32)
    packed = packed.astype(jnp.bfloat16).reshape(experts, capacity, model_width)
    summed, weight_row = expert_layer(
        packed, kernel, hot.T, expert_gate[0], expert_up[0], expert_down[0]
    )
    route_weight = weight_row[0]
    expert_out = jnp.dot(
        spread, summed.reshape(experts * capacity, model_width), preferred_element_type=jnp.float32
    )
    layer_out = (mixed + route_weight[:, None] * expert_out).astype(jnp.bfloat16)
    return (layer_out, route_weight)


def solution(mesh):
    in_specs = (
        P(("seq", "exp"), None),
        P(("seq", "exp"), None),
        P(("seq", "exp"), None),
        P(("seq", "exp"), None),
        P(("seq", "exp"), None),
        P(),
        P(),
        P(),
        P(),
        P(("seq", "exp"), None),
        P(("seq", "exp"), None, None),
        P(("seq", "exp"), None, None),
        P(("seq", "exp"), None, None),
    )
    out_specs = (P(("seq", "exp"), None), P(("seq", "exp")))
    return jax.shard_map(
        per_device, mesh=mesh, in_specs=in_specs, out_specs=out_specs, check_vma=False
    )
```

```python
import functools

import jax
import jax.numpy as jnp
from jax import lax
from jax.experimental import pallas as pl
from jax.experimental.pallas import tpu as pltpu
from jax.sharding import PartitionSpec as P

SINK_ITERS = 8
LANES = 128
MESH = pl.DeviceIdType.MESH


def place(flat):
    across = lax.axis_size("exp")
    return (flat // across, flat % across)


def own_index():
    return lax.axis_index("seq") * lax.axis_size("exp") + lax.axis_index("exp")


def device_count():
    return lax.axis_size("seq") * lax.axis_size("exp")


def meet_all(me, devices):
    barrier = pltpu.get_barrier_semaphore()

    @pl.loop(1, devices)
    def _(step):
        pl.semaphore_signal(
            barrier, inc=1, device_id=place((me + step) % devices), device_id_type=MESH
        )

    pl.semaphore_wait(barrier, devices - 1)


def per_lane(columns, group, head_size):
    count = LANES // head_size
    lane = lax.broadcasted_iota(jnp.int32, (1, LANES), 1)
    made = columns[:, group * count:group * count + 1]
    for at in range(1, count):
        head = group * count + at
        made = jnp.where(lane >= at * head_size, columns[:, head:head + 1], made)
    return made


def mixer_kernel(pieces, x_ref, residual_ref, b_ref, c_ref, sum_ref, sum_row_ref, weight_ref, weight_row_ref, skip_ref,
                 gain_ref, router_ref, chosen_ref, proj_hbm, packed_ref, kernel_ref, hot_ref, spread_ref, mixed_ref,
                 proj, states, entry, inner, scanned_out, normed_ref, own_factor,
                 arrived, totals, gathered, scanned, entered, entries,
                 factors, products, spans, go_send, go_recv, factor_send, factor_recv, up_send, up_recv,
                 span_send, span_recv, down_send, down_recv, back_send, back_recv, proj_sem):
    line, spot = lax.axis_index("seq"), lax.axis_index("exp")
    lines = lax.axis_size("seq")
    level, side = spot // 2, spot % 2
    mine = 2 * line + side
    near = 2 * lines
    levels = lax.axis_size("exp") // 2
    rows, cols = arrived.shape[2:]
    part = rows // levels
    length, width = x_ref.shape
    head_size = width // sum_ref.shape[1]
    lane_groups = width // LANES

    def near_place(peer):
        return (peer // 2, 2 * level + peer % 2)

    def far_place(peer):
        return (line, 2 * peer + side)

    def remote(src, dst, send, recv, device):
        return pltpu.make_async_remote_copy(
            src_ref=src, dst_ref=dst, send_sem=send, recv_sem=recv, device_id=device, device_id_type=MESH)

    def region(ref, piece, slot):
        return ref.at[pl.ds(piece * rows, rows), pl.ds(pl.multiple_of(slot * cols, cols), cols)]

    def go_copy(piece, peer, slot):
        return remote(region(states, piece, peer), arrived.at[piece, slot], go_send.at[piece, peer],
                      go_recv.at[piece, slot], near_place(peer))

    def factor_copy(peer, slot):
        return remote(own_factor.at[peer], factors.at[slot], factor_send.at[peer], factor_recv.at[slot],
                      near_place(peer))

    def up_copy(piece, peer, slot):
        return remote(totals.at[piece, peer], gathered.at[piece, slot], up_send.at[piece, peer],
                      up_recv.at[piece, slot], far_place(peer))

    def span_copy(peer, slot):
        return remote(products, spans.at[slot], span_send.at[peer], span_recv.at[slot], far_place(peer))

    def down_copy(piece, peer, slot):
        return remote(scanned.at[piece, peer], entered.at[piece, slot], down_send.at[piece, peer],
                      down_recv.at[piece, slot], far_place(peer))

    def back_copy(piece, peer, slot):
        return remote(entries.at[piece, peer], region(entry, piece, slot), back_send.at[piece, peer],
                      back_recv.at[piece, slot], near_place(peer))

    barrier = pltpu.get_barrier_semaphore()

    @pl.loop(1, near)
    def _(step):
        pl.semaphore_signal(barrier, inc=1, device_id=near_place((mine + step) % near), device_id_type=MESH)

    @pl.loop(1, levels)
    def _(step):
        pl.semaphore_signal(barrier, inc=1, device_id=far_place((level + step) % levels), device_id_type=MESH)

    load = pltpu.make_async_copy(proj_hbm, proj, proj_sem.at[0])
    load.start()

    sums, weight = sum_ref[...], weight_ref[...]
    last = sums[length - 1:length]
    tail_weight = jnp.exp(last - sums) * weight
    factor = jnp.exp(last)
    for group in range(lane_groups):
        slot, offset = group * LANES // cols, group * LANES % cols
        own_factor[slot, :, offset:offset + LANES] = per_lane(factor, group, head_size)
        tail_in = x_ref[:, group * LANES:(group + 1) * LANES].astype(jnp.float32) * per_lane(
            tail_weight, group, head_size)
        made = lax.dot_general(b_ref[...], tail_in.astype(jnp.bfloat16), (((0,), (0,)), ((), ())),
                               preferred_element_type=jnp.float32)
        states[:, group * LANES:(group + 1) * LANES] = made.astype(states.dtype)

    factors[mine] = own_factor[mine]
    for piece in range(pieces):
        arrived[piece, mine] = region(states, piece, mine)[...]
    pl.semaphore_wait(barrier, near + levels - 2)

    @pl.loop(1, near)
    def _(step):
        peer = (mine + step) % near
        factor_copy(peer, mine).start()
        go_copy(0, peer, mine).start()

    for piece in range(1, pieces):
        @pl.loop(1, near)
        def _(step):
            go_copy(piece, (mine + step) % near, mine).start()

    scores = lax.dot_general(c_ref[...], b_ref[...], (((1,), (1,)), ((), ())), preferred_element_type=jnp.float32)
    causal = lax.broadcasted_iota(jnp.int32, (length, length), 0) >= lax.broadcasted_iota(
        jnp.int32, (length, length), 1)
    scores = jnp.where(causal, scores, 0.0)

    def inside(first, stop):
        lane = lax.broadcasted_iota(jnp.int32, (1, LANES), 1)
        count = LANES // head_size
        for group in range(first, stop):
            columns = slice(group * LANES, (group + 1) * LANES)
            x = x_ref[:, columns]
            made = None
            for at in range(count):
                head = group * count + at
                distance = sums[:, head:head + 1] - sum_row_ref[head:head + 1]
                mix = jnp.exp(jnp.minimum(distance, 0.0)) * (weight_row_ref[head:head + 1] * scores)
                one = jnp.dot(mix.astype(jnp.bfloat16), x, preferred_element_type=jnp.float32)
                made = one if at == 0 else jnp.where(lane >= at * head_size, one, made)
            inner[:, columns] = made + skip_ref[:, columns] * x.astype(jnp.float32)

    def sorted_rows():
        chosen = chosen_ref[...]
        choices = hot_ref.shape[0]
        capacity = spread_ref.shape[0] // choices
        hot = (lax.broadcasted_iota(jnp.int32, (choices, length), 0) == chosen).astype(jnp.float32)
        hot_ref[...] = hot
        upto = (lax.broadcasted_iota(jnp.int32, (length, length), 0) <= lax.broadcasted_iota(
            jnp.int32, (length, length), 1)).astype(jnp.float32).astype(jnp.bfloat16)
        counts = jnp.dot(hot.astype(jnp.bfloat16), upto, preferred_element_type=jnp.float32)
        slot = jnp.sum(counts * hot, axis=0, keepdims=True).astype(jnp.int32) - 1
        position = chosen * capacity + slot
        spread_ref[...] = (lax.broadcasted_iota(jnp.int32, spread_ref.shape, 0) == position).astype(
            jnp.float32).astype(spread_ref.dtype)

    inside(0, lane_groups // 2)

    for piece in range(pieces):
        @pl.loop(1, near)
        def _(step):
            peer = (mine + near - step) % near
            if piece == 0:
                factor_copy(peer, peer).wait_recv()
            go_copy(piece, peer, peer).wait_recv()

        if piece == 0:
            @pl.loop(0, lines)
            def _(at):
                products[at] = factors[2 * at] * factors[2 * at + 1]

            spans[level] = products[...]

            @pl.loop(1, levels)
            def _(step):
                span_copy((level + step) % levels, level).start()

        @pl.loop(0, lines)
        def _(at):
            both = factors[2 * at + 1] * arrived[piece, 2 * at].astype(jnp.float32)
            both = both + arrived[piece, 2 * at + 1].astype(jnp.float32)
            totals[piece, :, at] = both.astype(totals.dtype).reshape(levels, part, cols)

        gathered[piece, level] = totals[piece, level]

        @pl.loop(1, levels)
        def _(step):
            up_copy(piece, (level + step) % levels, level).start()

    inside(lane_groups // 2, lane_groups)

    for piece in range(pieces):
        @pl.loop(1, levels)
        def _(step):
            peer = (level + levels - step) % levels
            if piece == 0:
                span_copy(peer, peer).wait_recv()
            up_copy(piece, peer, peer).wait_recv()

        def advance(k, state):
            at, floor = k // levels, k % levels
            scanned[piece, floor, at] = state.astype(scanned.dtype)
            return spans[floor, at] * state + gathered[piece, floor, at].astype(jnp.float32)

        lax.fori_loop(0, lines * levels, advance, jnp.zeros((part, cols), jnp.float32))
        entered[piece, level] = scanned[piece, level]

        @pl.loop(1, levels)
        def _(step):
            down_copy(piece, (level + step) % levels, level).start()

    sorted_rows()

    for piece in range(pieces):
        @pl.loop(1, levels)
        def _(step):
            peer = (level + levels - step) % levels
            down_copy(piece, peer, peer).wait_recv()

        @pl.loop(0, lines)
        def _(at):
            first = entered[piece, :, at].reshape(rows, cols)
            entries[piece, 2 * at] = first
            second = factors[2 * at] * first.astype(jnp.float32) + arrived[piece, 2 * at].astype(jnp.float32)
            entries[piece, 2 * at + 1] = second.astype(entries.dtype)

        @pl.loop(1, near)
        def _(step):
            back_copy(piece, (mine + step) % near, mine).start()

        region(entry, piece, mine)[...] = entries[piece, mine]

    load.wait()
    grown = jnp.exp(sums)

    @pl.loop(1, near)
    def _(step):
        peer = (mine + near - step) % near
        factor_copy(peer, peer).wait_send()
        for piece in range(pieces):
            go_copy(piece, peer, peer).wait_send()
            back_copy(piece, peer, peer).wait_recv()

    for group in range(lane_groups):
        columns = slice(group * LANES, (group + 1) * LANES)
        carried = jnp.dot(c_ref[...], entry[:, columns], preferred_element_type=jnp.float32)
        carried = per_lane(grown, group, head_size) * carried
        scanned_out[:, columns] = (inner[:, columns] + carried).astype(scanned_out.dtype)

    chunk = 512
    squares = jnp.zeros((length, 1), jnp.float32)
    for column in range(0, width, chunk):
        columns = slice(column, column + chunk)
        mixed = residual_ref[:, columns].astype(jnp.float32) + jnp.dot(
            scanned_out[...], proj[:, columns], preferred_element_type=jnp.float32)
        mixed_ref[:, columns] = mixed
        squares = squares + jnp.sum(mixed * mixed, axis=1, keepdims=True)
    scale = lax.rsqrt(squares / width + 1e-05)
    for column in range(0, width, chunk):
        columns = slice(column, column + chunk)
        normed = (mixed_ref[:, columns] * scale * gain_ref[:, columns]).astype(jnp.bfloat16)
        normed_ref[:, columns] = normed
        packed_ref[:, columns] = jnp.dot(
            spread_ref[...], normed, preferred_element_type=jnp.float32).astype(packed_ref.dtype)
    kernel_ref[...] = jnp.exp(lax.dot_general(
        router_ref[...], normed_ref[...], (((1,), (1,)), ((), ())), preferred_element_type=jnp.float32))

    @pl.loop(1, near)
    def _(step):
        peer = (mine + near - step) % near
        for piece in range(pieces):
            back_copy(piece, peer, peer).wait_send()

    @pl.loop(1, levels)
    def _(step):
        peer = (level + levels - step) % levels
        span_copy(peer, peer).wait_send()
        for piece in range(pieces):
            up_copy(piece, peer, peer).wait_send()
            down_copy(piece, peer, peer).wait_send()


def mixer(x, residual, b, c, sums, weight, skip_wide, gain, router, chosen, proj, slots):
    lines, levels = lax.axis_size("seq"), lax.axis_size("exp") // 2
    near = 2 * lines
    length, width = x.shape
    state_size = b.shape[1]
    choices = router.shape[1]
    model_width = proj.shape[1]
    pieces = max(1, min(2, state_size // (16 * levels)))
    rows, cols = state_size // pieces, width // near
    part = rows // levels
    dma = pltpu.SemaphoreType.DMA
    vmem = pl.BlockSpec(memory_space=pltpu.VMEM)
    flat = pltpu.VMEM((pieces, near, rows, cols), jnp.bfloat16)
    deep = pltpu.VMEM((pieces, levels, lines, part, cols), jnp.bfloat16)
    nears, fars = dma((pieces, near)), dma((pieces, levels))
    return pl.pallas_call(
        functools.partial(mixer_kernel, pieces),
        out_shape=(
            jax.ShapeDtypeStruct((slots, model_width), jnp.bfloat16),
            jax.ShapeDtypeStruct((choices, length), jnp.float32),
            jax.ShapeDtypeStruct((choices, length), jnp.float32),
            jax.ShapeDtypeStruct((slots, length), jnp.bfloat16),
            jax.ShapeDtypeStruct((length, model_width), jnp.float32),
        ),
        in_specs=[vmem] * 12 + [pl.BlockSpec(memory_space=pl.ANY)],
        out_specs=(vmem,) * 5,
        scratch_shapes=[
            pltpu.VMEM(proj.shape, jnp.bfloat16),
            pltpu.VMEM((state_size, width), jnp.bfloat16),
            pltpu.VMEM((state_size, width), jnp.bfloat16),
            pltpu.VMEM((length, width), jnp.float32),
            pltpu.VMEM((length, width), jnp.bfloat16),
            pltpu.VMEM((length, model_width), jnp.bfloat16),
            pltpu.VMEM((near, 1, cols), jnp.float32),
            flat, deep, deep, deep, deep, flat,
            pltpu.VMEM((near, 1, cols), jnp.float32),
            pltpu.VMEM((lines, 1, cols), jnp.float32),
            pltpu.VMEM((levels, lines, 1, cols), jnp.float32),
            nears, nears, dma((near,)), dma((near,)), fars, fars,
            dma((levels,)), dma((levels,)), fars, fars, nears, nears, dma((1,)),
        ],
        compiler_params=pltpu.CompilerParams(
            collective_id=0, has_side_effects=True, vmem_limit_bytes=32 << 20
        ),
        name="mixer",
    )(x, residual, b, c, sums, sums.T, weight, weight.T, skip_wide, gain[None, :], router.T, chosen, proj)


def expert_kernel(devices, group, lag, tail, packed_ref, kernel_ref, hot_ref, spread_ref, mixed_ref, gate_hbm, up_hbm,
                  down_hbm, layer_ref, weight_ref, out_ref,
                  table_ref, rows, halves, partial, summed, gate, up, down, block,
                  go_send, go_recv, pass_send, pass_recv, swap_send, swap_recv, back_send, back_recv,
                  near_send, near_recv, far_send, far_recv, own_sem, weight_sem):
    line, spot = lax.axis_index("seq"), lax.axis_index("exp")
    lines, spots = lax.axis_size("seq"), lax.axis_size("exp")
    me = line * spots + spot
    side, mine = me % 2, me // 2
    experts = devices // 2
    partner = me + 1 - 2 * side
    capacity, width = packed_ref.shape[1:]
    turns = experts // group

    def remote(src, dst, send, recv, device):
        return pltpu.make_async_remote_copy(
            src_ref=src, dst_ref=dst, send_sem=send, recv_sem=recv, device_id=device, device_id_type=MESH)

    def row_copy(other, slot):
        return remote(packed_ref.at[other], rows.at[side, slot], go_send.at[other], go_recv.at[slot],
                      place(2 * other + side))

    def pass_copy(at, slot):
        return remote(rows.at[side, slot], rows.at[at, slot], pass_send.at[slot], pass_recv.at[slot],
                      place(partner))

    def swap_copy(slot):
        return remote(halves.at[1 - side, slot], partial.at[slot], swap_send.at[slot], swap_recv.at[slot],
                      place(partner))

    def back_copy(other, slot):
        return remote(summed.at[other], out_ref.at[slot], back_send.at[other], back_recv.at[slot],
                      place(2 * other + side))

    def near_copy(other, slot):
        return remote(kernel_ref, table_ref.at[line, slot], near_send.at[other], near_recv.at[slot],
                      (line, other))

    def far_copy(other, slot):
        return remote(table_ref.at[line], table_ref.at[slot], far_send.at[other], far_recv.at[slot],
                      (other, spot))

    own_rows = pltpu.make_async_copy(packed_ref.at[mine], rows.at[side, mine], own_sem.at[0])
    own_table = pltpu.make_async_copy(kernel_ref, table_ref.at[line, spot], own_sem.at[1])
    own_rows.start()
    own_table.start()
    loads = [
        pltpu.make_async_copy(gate_hbm, gate, weight_sem.at[0]),
        pltpu.make_async_copy(up_hbm, up, weight_sem.at[1]),
        pltpu.make_async_copy(down_hbm, down, weight_sem.at[2]),
    ]
    for load in loads:
        load.start()
    meet_all(me, devices)

    floors = spots // 2
    row, floor = mine // floors, mine % floors

    def target(k):
        return ((row + k % lines) % lines) * floors + (floor + k // lines) % floors

    def source(k):
        return ((row + lines - k % lines) % lines) * floors + (floor + floors - k // lines) % floors

    @pl.loop(1, spots)
    def _(step):
        near_copy((spot + step) % spots, spot).start()

    @pl.loop(1, experts)
    def _(k):
        row_copy(target(k), mine).start()

    own_rows.wait()
    pass_copy(side, mine).start()

    @pl.loop(0, turns + lag + tail)
    def _(turn):
        @pl.when(turn < turns)
        def _():
            @pl.loop(0, group)
            def _(at):
                k = turn * group + at

                @pl.when(k > 0)
                def _():
                    row_copy(source(k), source(k)).wait_recv()
                    pass_copy(side, source(k)).start()

        @pl.when(turn == 0)
        def _():
            for load in loads:
                load.wait()

        @pl.when((turn >= lag) & (turn < turns + lag))
        def _():
            first = (turn - lag) * group

            @pl.loop(0, group)
            def _(at):
                pass_copy(1 - side, source(first + at)).wait_recv()

            sources = [source(first + at) for at in range(group)]
            places = [(k, src, (k * group + at) * capacity)
                      for k in range(2) for at, src in enumerate(sources)]
            for k, src, start in places:
                block[start:start + capacity] = rows[k, src]
            taken = block[...]
            across = (((1,), (1,)), ((), ()))
            gate_val = lax.dot_general(taken, gate[...], across, preferred_element_type=jnp.float32)
            up_val = lax.dot_general(taken, up[...], across, preferred_element_type=jnp.float32)
            hidden = (gate_val / (1.0 + jnp.exp(-gate_val)) * up_val).astype(jnp.bfloat16)
            piece = 512
            for column in range(0, width, piece):
                made = jnp.dot(hidden, down[:, column:column + piece], preferred_element_type=jnp.float32)
                made = made.astype(halves.dtype)
                for k, src, start in places:
                    halves[k, src, :, column:column + piece] = made[start:start + capacity]

            @pl.loop(0, group)
            def _(at):
                swap_copy(source(first + at)).start()

        @pl.when(turn >= lag + tail)
        def _():
            @pl.loop(0, group)
            def _(at):
                k = (turn - lag - tail) * group + at
                src = source(k)
                swap_copy(src).wait_recv()
                summed[src] = (
                    halves[side, src].astype(jnp.float32) + partial[src].astype(jnp.float32)
                ).astype(summed.dtype)

                @pl.when(k > 0)
                def _():
                    back_copy(src, mine).start()

        @pl.when(turn == turns // 2)
        def _():
            own_table.wait()

            @pl.loop(1, spots)
            def _(step):
                near_copy((spot + step) % spots, (spot + step) % spots).wait_recv()

            @pl.loop(1, lines)
            def _(step):
                far_copy((line + step) % lines, line).start()

    own_out = pltpu.make_async_copy(summed.at[mine], out_ref.at[mine], own_sem.at[0])
    own_out.start()

    @pl.loop(1, lines)
    def _(step):
        other = (line + step) % lines
        far_copy(other, other).wait_recv()
        far_copy(other, other).wait_send()

    choices, length = kernel_ref.shape

    def sweep(_, column):
        def add(at, totals):
            part = table_ref[at]
            row_scale = 1.0 / jnp.sum(part * column[None], axis=1, keepdims=True)
            return totals + jnp.sum(part * row_scale, axis=0)

        totals = lax.fori_loop(0, lines, add, jnp.zeros((choices, length), jnp.float32))
        return 1.0 / jnp.sum(totals, axis=1, keepdims=True)

    column = lax.fori_loop(0, SINK_ITERS, sweep, jnp.ones((choices, 1), jnp.float32))
    weighted = kernel_ref[...] * column
    picked = jnp.sum(jnp.where(hot_ref[...] > 0.0, weighted, 0.0), axis=0, keepdims=True)
    weight = choices * picked / jnp.sum(weighted, axis=0, keepdims=True)
    weight_ref[...] = weight
    same = lax.broadcasted_iota(jnp.int32, (length, length), 0) == lax.broadcasted_iota(
        jnp.int32, (length, length), 1)
    weight_column = jnp.sum(jnp.where(same, weight, 0.0), axis=1, keepdims=True)

    @pl.loop(1, spots)
    def _(step):
        near_copy((spot + step) % spots, spot).wait_send()

    @pl.loop(0, experts)
    def _(step):
        pass_copy(side, step).wait_send()
        swap_copy(step).wait_send()

    @pl.loop(1, experts)
    def _(step):
        other = (mine + step) % experts
        row_copy(other, other).wait_send()
        back_copy(other, other).wait_recv()
        back_copy(other, other).wait_send()

    own_out.wait()
    for column in range(0, width, 512):
        columns = slice(column, column + 512)
        made = lax.dot_general(spread_ref[...], out_ref[:, :, columns].reshape(experts * capacity, 512),
                               (((0,), (0,)), ((), ())), preferred_element_type=jnp.float32)
        layer_ref[:, columns] = (mixed_ref[:, columns] + weight_column * made).astype(layer_ref.dtype)


def expert_layer(packed, kernel, hot, spread, mixed, gate_half, up_half, down_half):
    devices = device_count()
    lines, spots = lax.axis_size("seq"), lax.axis_size("exp")
    experts, capacity, width = packed.shape
    hidden_units = down_half.shape[0]
    group, lag, tail = 2, 1, 1
    dma = pltpu.SemaphoreType.DMA
    vmem = pl.BlockSpec(memory_space=pltpu.VMEM)
    anywhere = pl.BlockSpec(memory_space=pl.ANY)
    single = pltpu.VMEM((experts, capacity, width), packed.dtype)
    double = pltpu.VMEM((2, experts, capacity, width), packed.dtype)
    weights = pltpu.VMEM((hidden_units, width), packed.dtype)
    each = dma((experts,))
    return pl.pallas_call(
        functools.partial(expert_kernel, devices, group, lag, tail),
        out_shape=(
            jax.ShapeDtypeStruct(mixed.shape, packed.dtype),
            jax.ShapeDtypeStruct((1, kernel.shape[1]), kernel.dtype),
        ),
        in_specs=[vmem] * 5 + [anywhere] * 3,
        out_specs=(vmem, vmem),
        scratch_shapes=[
            single, pltpu.VMEM((lines, spots, *kernel.shape), kernel.dtype),
            double, double, single, single, weights, weights, weights,
            pltpu.VMEM((2 * group * capacity, width), packed.dtype),
            each, each, each, each, each, each, each, each,
            dma((spots,)), dma((spots,)), dma((lines,)), dma((lines,)), dma((2,)), dma((3,)),
        ],
        compiler_params=pltpu.CompilerParams(collective_id=1, has_side_effects=True),
        name="expert_layer",
    )(packed, kernel, hot, spread, mixed, gate_half.T, up_half.T, down_half)


def widen(per_head, width):
    return jnp.repeat(per_head, width // per_head.shape[-1], axis=-1)


def per_device(
    residual_in,
    ssm_input,
    ssm_b,
    ssm_c,
    log_decay,
    skip_gain,
    out_proj,
    norm_gain,
    router,
    assignment,
    expert_gate,
    expert_up,
    expert_down,
):
    length, row_width = ssm_input.shape
    model_width = residual_in.shape[1]
    experts = router.shape[1]
    capacity = max(16, 2 * length // experts)
    packed, kernel, hot, spread, mixed = mixer(
        ssm_input, residual_in, ssm_b, ssm_c, jnp.cumsum(log_decay, axis=0),
        jnp.sqrt(-jnp.expm1(2.0 * log_decay)), widen(skip_gain, row_width)[None, :], norm_gain, router,
        assignment.T, out_proj, experts * capacity)
    layer_out, weight_row = expert_layer(
        packed.reshape(experts, capacity, model_width), kernel, hot, spread, mixed,
        expert_gate[0], expert_up[0], expert_down[0])
    return (layer_out, weight_row[0])


def solution(mesh):
    in_specs = (
        P(("seq", "exp"), None),
        P(("seq", "exp"), None),
        P(("seq", "exp"), None),
        P(("seq", "exp"), None),
        P(("seq", "exp"), None),
        P(),
        P(),
        P(),
        P(),
        P(("seq", "exp"), None),
        P(("seq", "exp"), None, None),
        P(("seq", "exp"), None, None),
        P(("seq", "exp"), None, None),
    )
    out_specs = (P(("seq", "exp"), None), P(("seq", "exp")))
    return jax.shard_map(
        per_device, mesh=mesh, in_specs=in_specs, out_specs=out_specs, check_vma=False
    )
```

```python
import functools

import jax
import jax.numpy as jnp
from jax import lax
from jax.experimental import pallas as pl
from jax.experimental.pallas import tpu as pltpu
from jax.sharding import PartitionSpec as P

SINK_ITERS = 8
LANES = 128
MESH = pl.DeviceIdType.MESH


def place(flat):
    across = lax.axis_size("exp")
    return (flat // across, flat % across)


def own_index():
    return lax.axis_index("seq") * lax.axis_size("exp") + lax.axis_index("exp")


def device_count():
    return lax.axis_size("seq") * lax.axis_size("exp")


def per_lane(columns, group, head_size):
    count = LANES // head_size
    lane = lax.broadcasted_iota(jnp.int32, (1, LANES), 1)
    made = columns[:, group * count:group * count + 1]
    for at in range(1, count):
        head = group * count + at
        made = jnp.where(lane >= at * head_size, columns[:, head:head + 1], made)
    return made


def one_less_exp(y):
    series = 1.0
    for order in range(8, 1, -1):
        series = 1.0 + y / order * series
    return jnp.where(y > -0.5, -y * series, 1.0 - jnp.exp(y))


def layer_kernel(pieces, batch, lag, tail, x_hbm, residual_hbm, b_hbm, c_hbm, decay_hbm, skip_hbm, gain_hbm, router_hbm,
                 chosen_hbm, proj_hbm, gate_hbm, up_hbm, down_hbm, layer_ref, weight_ref,
                 x_ref, residual_ref, b_ref, c_ref, decay_ref, skip_ref, gain_ref, router_ref, chosen_ref,
                 packed_ref, kernel_ref, hot_ref, spread_ref, mixed_ref,
                 states, entry, inner, scanned_out, normed_ref, own_factor,
                 arrived, totals, gathered, scanned, entered, entries, factors, products, spans,
                 out_ref, table_ref, rows_ref, halves, partial, gate, up, down, block,
                 go_send, go_recv, factor_send, factor_recv, up_send, up_recv,
                 span_send, span_recv, down_send, down_recv, back_send, back_recv,
                 row_send, row_recv, pass_send, pass_recv, swap_send, swap_recv, home_send, home_recv,
                 near_send, near_recv, far_send, far_recv, own_sem, load_sem):
    line, spot = lax.axis_index("seq"), lax.axis_index("exp")
    lines = lax.axis_size("seq")
    level, side = spot // 2, spot % 2
    me = own_index()
    devices = device_count()
    slot_of = 2 * line + side
    near = 2 * lines
    levels = lax.axis_size("exp") // 2
    rows, cols = arrived.shape[2:]
    part = rows // levels
    length, width = x_ref.shape
    head_size = width // decay_ref.shape[0]
    lane_groups = width // LANES

    def near_place(peer):
        return (peer // 2, 2 * level + peer % 2)

    def far_place(peer):
        return (line, 2 * peer + side)

    def remote(src, dst, send, recv, device):
        return pltpu.make_async_remote_copy(
            src_ref=src, dst_ref=dst, send_sem=send, recv_sem=recv, device_id=device, device_id_type=MESH)

    def region(ref, piece, slot):
        return ref.at[pl.ds(piece * rows, rows), pl.ds(pl.multiple_of(slot * cols, cols), cols)]

    def go_copy(piece, peer, slot):
        return remote(region(states, piece, peer), arrived.at[piece, slot], go_send.at[piece, peer],
                      go_recv.at[piece, slot], near_place(peer))

    def factor_copy(peer, slot):
        return remote(own_factor.at[peer], factors.at[slot], factor_send.at[peer], factor_recv.at[slot],
                      near_place(peer))

    def up_copy(piece, peer, slot):
        return remote(totals.at[piece, peer], gathered.at[piece, slot], up_send.at[piece, peer],
                      up_recv.at[piece, slot], far_place(peer))

    def span_copy(peer, slot):
        return remote(products, spans.at[slot], span_send.at[peer], span_recv.at[slot], far_place(peer))

    def down_copy(piece, peer, slot):
        return remote(scanned.at[piece, peer], entered.at[piece, slot], down_send.at[piece, peer],
                      down_recv.at[piece, slot], far_place(peer))

    def back_copy(piece, peer, slot):
        return remote(entries.at[piece, peer], region(entry, piece, slot), back_send.at[piece, peer],
                      back_recv.at[piece, slot], near_place(peer))

    barrier = pltpu.get_barrier_semaphore()

    @pl.loop(1, devices)
    def _(step):
        pl.semaphore_signal(
            barrier, inc=1, device_id=place((me + step) % devices), device_id_type=MESH
        )

    proj = halves.at[pl.ds(0, proj_hbm.shape[0])]
    loads = [
        pltpu.make_async_copy(src, dst, load_sem.at[at])
        for at, (src, dst) in enumerate((
            (decay_hbm, decay_ref), (b_hbm, b_ref), (x_hbm, x_ref), (c_hbm, c_ref), (skip_hbm, skip_ref),
            (chosen_hbm, chosen_ref), (gain_hbm, gain_ref), (router_hbm, router_ref), (residual_hbm, residual_ref),
            (proj_hbm, proj), (gate_hbm, gate), (up_hbm, up), (down_hbm, down),
        ))
    ]
    for load in loads:
        load.start()

    before = (lax.broadcasted_iota(jnp.int32, (length, length), 0) <= lax.broadcasted_iota(
        jnp.int32, (length, length), 1)).astype(jnp.float32)
    loads[0].wait()
    decay_row = decay_ref[...]
    sum_row = jnp.dot(decay_row, before, precision=lax.Precision.HIGHEST, preferred_element_type=jnp.float32)
    weight_row = jnp.sqrt(one_less_exp(2.0 * decay_row))
    sums = sum_row.T
    last = sums[length - 1:length]
    tail_weight = jnp.exp(last - sums) * weight_row.T
    factor = jnp.exp(last)
    for load in loads[1:6]:
        load.wait()
    for group in range(lane_groups):
        slot, offset = group * LANES // cols, group * LANES % cols
        own_factor[slot, :, offset:offset + LANES] = per_lane(factor, group, head_size)
        tail_in = x_ref[:, group * LANES:(group + 1) * LANES].astype(jnp.float32) * per_lane(
            tail_weight, group, head_size)
        made = lax.dot_general(b_ref[...], tail_in.astype(jnp.bfloat16), (((0,), (0,)), ((), ())),
                               preferred_element_type=jnp.float32)
        states[:, group * LANES:(group + 1) * LANES] = made.astype(states.dtype)

    factors[slot_of] = own_factor[slot_of]
    for piece in range(pieces):
        arrived[piece, slot_of] = region(states, piece, slot_of)[...]
    pl.semaphore_wait(barrier, devices - 1)

    @pl.loop(1, near)
    def _(step):
        peer = (slot_of + step) % near
        factor_copy(peer, slot_of).start()
        go_copy(0, peer, slot_of).start()

    for piece in range(1, pieces):
        @pl.loop(1, near)
        def _(step):
            go_copy(piece, (slot_of + step) % near, slot_of).start()

    scores = lax.dot_general(c_ref[...], b_ref[...], (((1,), (1,)), ((), ())), preferred_element_type=jnp.float32)
    causal = lax.broadcasted_iota(jnp.int32, (length, length), 0) >= lax.broadcasted_iota(
        jnp.int32, (length, length), 1)
    scores = jnp.where(causal, scores, 0.0)

    skip = skip_ref[...]

    def inside(first, stop):
        lane = lax.broadcasted_iota(jnp.int32, (1, LANES), 1)
        count = LANES // head_size
        for group in range(first, stop):
            columns = slice(group * LANES, (group + 1) * LANES)
            x = x_ref[:, columns]
            made = None
            for at in range(count):
                head = group * count + at
                distance = sums[:, head:head + 1] - sum_row[head:head + 1]
                mix = jnp.exp(jnp.minimum(distance, 0.0)) * (weight_row[head:head + 1] * scores)
                one = jnp.dot(mix.astype(jnp.bfloat16), x, preferred_element_type=jnp.float32)
                made = one if at == 0 else jnp.where(lane >= at * head_size, one, made)
            inner[:, columns] = made + per_lane(skip, group, head_size) * x.astype(jnp.float32)

    def sorted_rows():
        chosen = chosen_ref[...]
        choices = hot_ref.shape[0]
        capacity = spread_ref.shape[0] // choices
        hot = (lax.broadcasted_iota(jnp.int32, (choices, length), 0) == chosen).astype(jnp.float32)
        hot_ref[...] = hot
        counts = jnp.dot(hot.astype(jnp.bfloat16), before.astype(jnp.bfloat16), preferred_element_type=jnp.float32)
        slot = jnp.sum(counts * hot, axis=0, keepdims=True).astype(jnp.int32) - 1
        position = chosen * capacity + slot
        spread_ref[...] = (lax.broadcasted_iota(jnp.int32, spread_ref.shape, 0) == position).astype(
            jnp.float32).astype(spread_ref.dtype)

    inside(0, lane_groups // 2)

    for piece in range(pieces):
        @pl.loop(1, near)
        def _(step):
            peer = (slot_of + near - step) % near
            if piece == 0:
                factor_copy(peer, peer).wait_recv()
            go_copy(piece, peer, peer).wait_recv()

        if piece == 0:
            @pl.loop(0, lines)
            def _(at):
                products[at] = factors[2 * at] * factors[2 * at + 1]

            spans[level] = products[...]

            @pl.loop(1, levels)
            def _(step):
                span_copy((level + step) % levels, level).start()

        @pl.loop(0, lines)
        def _(at):
            both = factors[2 * at + 1] * arrived[piece, 2 * at].astype(jnp.float32)
            both = both + arrived[piece, 2 * at + 1].astype(jnp.float32)
            totals[piece, :, at] = both.astype(totals.dtype).reshape(levels, part, cols)

        gathered[piece, level] = totals[piece, level]

        @pl.loop(1, levels)
        def _(step):
            up_copy(piece, (level + step) % levels, level).start()

    inside(lane_groups // 2, lane_groups)

    for piece in range(pieces):
        @pl.loop(1, levels)
        def _(step):
            peer = (level + levels - step) % levels
            if piece == 0:
                span_copy(peer, peer).wait_recv()
            up_copy(piece, peer, peer).wait_recv()

        def advance(k, state):
            at, floor = k // levels, k % levels
            scanned[piece, floor, at] = state.astype(scanned.dtype)
            return spans[floor, at] * state + gathered[piece, floor, at].astype(jnp.float32)

        lax.fori_loop(0, lines * levels, advance, jnp.zeros((part, cols), jnp.float32))
        entered[piece, level] = scanned[piece, level]

        @pl.loop(1, levels)
        def _(step):
            down_copy(piece, (level + step) % levels, level).start()

    sorted_rows()

    for piece in range(pieces):
        @pl.loop(1, levels)
        def _(step):
            peer = (level + levels - step) % levels
            down_copy(piece, peer, peer).wait_recv()

        @pl.loop(0, lines)
        def _(at):
            first = entered[piece, :, at].reshape(rows, cols)
            entries[piece, 2 * at] = first
            second = factors[2 * at] * first.astype(jnp.float32) + arrived[piece, 2 * at].astype(jnp.float32)
            entries[piece, 2 * at + 1] = second.astype(entries.dtype)

        @pl.loop(1, near)
        def _(step):
            back_copy(piece, (slot_of + step) % near, slot_of).start()

        region(entry, piece, slot_of)[...] = entries[piece, slot_of]

    for load in loads[6:10]:
        load.wait()
    grown = jnp.exp(sums)

    @pl.loop(1, near)
    def _(step):
        peer = (slot_of + near - step) % near
        factor_copy(peer, peer).wait_send()
        for piece in range(pieces):
            go_copy(piece, peer, peer).wait_send()
            back_copy(piece, peer, peer).wait_recv()

    for group in range(lane_groups):
        columns = slice(group * LANES, (group + 1) * LANES)
        carried = jnp.dot(c_ref[...], entry[:, columns], preferred_element_type=jnp.float32)
        carried = per_lane(grown, group, head_size) * carried
        scanned_out[:, columns] = (inner[:, columns] + carried).astype(scanned_out.dtype)

    chunk = 512
    squares = jnp.zeros((length, 1), jnp.float32)
    for column in range(0, width, chunk):
        columns = slice(column, column + chunk)
        mixed = residual_ref[:, columns].astype(jnp.float32) + jnp.dot(
            scanned_out[...], proj[:, columns], preferred_element_type=jnp.float32)
        mixed_ref[:, columns] = mixed
        squares = squares + jnp.sum(mixed * mixed, axis=1, keepdims=True)
    scale = lax.rsqrt(squares / width + 1e-05)
    for column in range(0, width, chunk):
        columns = slice(column, column + chunk)
        normed = (mixed_ref[:, columns] * scale * gain_ref[:, columns]).astype(jnp.bfloat16)
        normed_ref[:, columns] = normed
        made = jnp.dot(spread_ref[...], normed, preferred_element_type=jnp.float32)
        packed_ref[:, :, columns] = made.astype(packed_ref.dtype).reshape(*packed_ref.shape[:2], chunk)
    kernel_ref[...] = jnp.exp(lax.dot_general(
        router_ref[...], normed_ref[...], (((1,), (1,)), ((), ())), preferred_element_type=jnp.float32))

    spots = lax.axis_size("exp")
    mine = me // 2
    experts = devices // 2
    partner = me + 1 - 2 * side
    capacity, width = packed_ref.shape[1:]

    def half(at, slot):
        return halves.at[pl.ds(pl.multiple_of((at * experts + slot) * capacity, capacity), capacity)]
    turns = experts // batch

    def row_copy(other, slot):
        return remote(packed_ref.at[other], rows_ref.at[side, slot], row_send.at[other], row_recv.at[slot],
                      place(2 * other + side))

    def pass_copy(at, slot):
        return remote(rows_ref.at[side, slot], rows_ref.at[at, slot], pass_send.at[slot], pass_recv.at[slot],
                      place(partner))

    def swap_copy(slot):
        return remote(half(1 - side, slot), partial.at[slot], swap_send.at[slot], swap_recv.at[slot],
                      place(partner))

    def home_copy(other, slot):
        return remote(half(side, other), out_ref.at[slot], home_send.at[other], home_recv.at[slot],
                      place(2 * other + side))

    def near_copy(other, slot):
        return remote(kernel_ref, table_ref.at[line, slot], near_send.at[other], near_recv.at[slot],
                      (line, other))

    def far_copy(other, slot):
        return remote(table_ref.at[line], table_ref.at[slot], far_send.at[other], far_recv.at[slot],
                      (other, spot))

    own_rows = pltpu.make_async_copy(packed_ref.at[mine], rows_ref.at[side, mine], own_sem.at[0])
    own_table = pltpu.make_async_copy(kernel_ref, table_ref.at[line, spot], own_sem.at[1])
    own_rows.start()
    own_table.start()
    floors = spots // 2
    row, floor = mine // floors, mine % floors

    def target(k):
        return ((row + k % lines) % lines) * floors + (floor + k // lines) % floors

    def source(k):
        return ((row + lines - k % lines) % lines) * floors + (floor + floors - k // lines) % floors

    @pl.loop(1, spots)
    def _(step):
        near_copy((spot + step) % spots, spot).start()

    @pl.loop(1, experts)
    def _(k):
        row_copy(target(k), mine).start()

    own_rows.wait()
    pass_copy(side, mine).start()

    @pl.loop(0, turns + lag + tail)
    def _(turn):
        @pl.when(turn < turns)
        def _():
            @pl.loop(0, batch)
            def _(at):
                k = turn * batch + at

                @pl.when(k > 0)
                def _():
                    row_copy(source(k), source(k)).wait_recv()
                    pass_copy(side, source(k)).start()

        @pl.when(turn == 0)
        def _():
            for load in loads[10:]:
                load.wait()

        @pl.when((turn >= lag) & (turn < turns + lag))
        def _():
            first = (turn - lag) * batch

            @pl.loop(0, batch)
            def _(at):
                pass_copy(1 - side, source(first + at)).wait_recv()

            sources = [source(first + at) for at in range(batch)]
            places = [(k, src, (k * batch + at) * capacity)
                      for k in range(2) for at, src in enumerate(sources)]
            for k, src, start in places:
                block[start:start + capacity] = rows_ref[k, src]
            taken = block[...]
            across = (((1,), (1,)), ((), ()))
            gate_val = lax.dot_general(taken, gate[...], across, preferred_element_type=jnp.float32)
            up_val = lax.dot_general(taken, up[...], across, preferred_element_type=jnp.float32)
            hidden = (gate_val / (1.0 + jnp.exp(-gate_val)) * up_val).astype(jnp.bfloat16)
            piece = 512
            for column in range(0, width, piece):
                made = jnp.dot(hidden, down[:, column:column + piece], preferred_element_type=jnp.float32)
                made = made.astype(halves.dtype)
                for k, src, start in places:
                    half(k, src)[:, column:column + piece] = made[start:start + capacity]

            @pl.loop(0, batch)
            def _(at):
                swap_copy(source(first + at)).start()

        @pl.when(turn >= lag + tail)
        def _():
            @pl.loop(0, batch)
            def _(at):
                k = (turn - lag - tail) * batch + at
                src = source(k)
                swap_copy(src).wait_recv()
                half(side, src)[...] = (
                    half(side, src)[...].astype(jnp.float32) + partial[src].astype(jnp.float32)
                ).astype(halves.dtype)

                @pl.when(k > 0)
                def _():
                    home_copy(src, mine).start()

        @pl.when(turn == turns // 2)
        def _():
            own_table.wait()

            @pl.loop(1, spots)
            def _(step):
                near_copy((spot + step) % spots, (spot + step) % spots).wait_recv()

            @pl.loop(1, lines)
            def _(step):
                far_copy((line + step) % lines, line).start()

    own_out = pltpu.make_async_copy(half(side, mine), out_ref.at[mine], own_sem.at[0])
    own_out.start()

    @pl.loop(1, lines)
    def _(step):
        other = (line + step) % lines
        far_copy(other, other).wait_recv()
        far_copy(other, other).wait_send()

    choices = kernel_ref.shape[0]

    def sweep(_, column):
        def add(at, totals):
            part = table_ref[at]
            row_scale = 1.0 / jnp.sum(part * column[None], axis=1, keepdims=True)
            return totals + jnp.sum(part * row_scale, axis=0)

        totals = lax.fori_loop(0, lines, add, jnp.zeros((choices, length), jnp.float32))
        return 1.0 / jnp.sum(totals, axis=1, keepdims=True)

    column = lax.fori_loop(0, SINK_ITERS, sweep, jnp.ones((choices, 1), jnp.float32))
    weighted = kernel_ref[...] * column
    picked = jnp.sum(jnp.where(hot_ref[...] > 0.0, weighted, 0.0), axis=0, keepdims=True)
    weight = choices * picked / jnp.sum(weighted, axis=0, keepdims=True)
    weight_ref[...] = weight
    same = lax.broadcasted_iota(jnp.int32, (length, length), 0) == lax.broadcasted_iota(
        jnp.int32, (length, length), 1)
    weight_column = jnp.sum(jnp.where(same, weight, 0.0), axis=1, keepdims=True)

    @pl.loop(1, spots)
    def _(step):
        near_copy((spot + step) % spots, spot).wait_send()

    @pl.loop(0, experts)
    def _(step):
        pass_copy(side, step).wait_send()
        swap_copy(step).wait_send()

    @pl.loop(1, experts)
    def _(step):
        other = (mine + step) % experts
        row_copy(other, other).wait_send()
        home_copy(other, other).wait_recv()
        home_copy(other, other).wait_send()

    own_out.wait()
    for column in range(0, width, 512):
        columns = slice(column, column + 512)
        made = lax.dot_general(spread_ref[...], out_ref[:, :, columns].reshape(experts * capacity, 512),
                               (((0,), (0,)), ((), ())), preferred_element_type=jnp.float32)
        layer_ref[:, columns] = (mixed_ref[:, columns] + weight_column * made).astype(layer_ref.dtype)

    @pl.loop(1, near)
    def _(step):
        peer = (slot_of + near - step) % near
        for piece in range(pieces):
            back_copy(piece, peer, peer).wait_send()

    @pl.loop(1, levels)
    def _(step):
        peer = (level + levels - step) % levels
        span_copy(peer, peer).wait_send()
        for piece in range(pieces):
            up_copy(piece, peer, peer).wait_send()
            down_copy(piece, peer, peer).wait_send()


def layer(x, residual, b, c, decay, skip, gain, router, assignment, proj, gate_half, up_half, down_half):
    devices = device_count()
    lines, spots = lax.axis_size("seq"), lax.axis_size("exp")
    levels, near, experts = spots // 2, 2 * lines, devices // 2
    length, width = x.shape
    state_size = b.shape[1]
    choices = router.shape[1]
    model_width = proj.shape[1]
    hidden_units = down_half.shape[0]
    capacity = max(16, 2 * length // choices)
    pieces = max(1, min(2, state_size // (16 * levels)))
    rows, cols = state_size // pieces, width // near
    part = rows // levels
    group, lag, tail = 2, 1, 1
    dma = pltpu.SemaphoreType.DMA
    vmem = pl.BlockSpec(memory_space=pltpu.VMEM)

    def half_words(*shape):
        return pltpu.VMEM(shape, jnp.bfloat16)

    def words(*shape):
        return pltpu.VMEM(shape, jnp.float32)

    flat = half_words(pieces, near, rows, cols)
    deep = half_words(pieces, levels, lines, part, cols)
    single = half_words(experts, capacity, model_width)
    weights = half_words(hidden_units, model_width)
    nears, fars, each = dma((pieces, near)), dma((pieces, levels)), dma((experts,))
    heads = decay.shape[1]
    return pl.pallas_call(
        functools.partial(layer_kernel, pieces, group, lag, tail),
        out_shape=(
            jax.ShapeDtypeStruct((length, model_width), jnp.bfloat16),
            jax.ShapeDtypeStruct((1, length), jnp.float32),
        ),
        in_specs=[pl.BlockSpec(memory_space=pl.ANY)] * 13,
        out_specs=(vmem, vmem),
        scratch_shapes=[
            half_words(length, width), half_words(length, model_width), half_words(length, state_size),
            half_words(length, state_size), words(heads, length), words(1, heads), words(1, model_width),
            half_words(choices, model_width), pltpu.VMEM((1, length), jnp.int32),
            single, words(choices, length), words(choices, length), half_words(choices * capacity, length),
            words(length, model_width),
            half_words(state_size, width), half_words(state_size, width), words(length, width),
            half_words(length, width), half_words(length, model_width), words(near, 1, cols),
            flat, deep, deep, deep, deep, flat, words(near, 1, cols), words(lines, 1, cols),
            words(levels, lines, 1, cols),
            single, words(lines, spots, choices, length), half_words(2, experts, capacity, model_width),
            half_words(max(2 * experts * capacity, width), model_width), single, weights, weights, weights,
            half_words(2 * group * capacity, model_width),
            nears, nears, dma((near,)), dma((near,)), fars, fars,
            dma((levels,)), dma((levels,)), fars, fars, nears, nears,
            each, each, each, each, each, each, each, each,
            dma((spots,)), dma((spots,)), dma((lines,)), dma((lines,)), dma((2,)), dma((13,)),
        ],
        compiler_params=pltpu.CompilerParams(
            collective_id=0, has_side_effects=True, vmem_limit_bytes=60 << 20
        ),
        name="layer",
    )(x, residual, b, c, decay.T, skip[None, :], gain[None, :], router.T, assignment.T, proj,
      gate_half.T, up_half.T, down_half)


def hand_over_kernel(layer_ref, weight_ref, layer_out, weight_out):
    layer_out[...] = layer_ref[...]
    weight_out[...] = weight_ref[...]


def hand_over(layer_out, weight):
    vmem = pl.BlockSpec(memory_space=pltpu.VMEM)
    return pl.pallas_call(
        hand_over_kernel,
        out_shape=(
            jax.ShapeDtypeStruct(layer_out.shape, layer_out.dtype),
            jax.ShapeDtypeStruct(weight.shape, weight.dtype),
        ),
        in_specs=[vmem, vmem],
        out_specs=(vmem, vmem),
        name="hand_over",
    )(layer_out, weight)


def per_device(
    residual_in,
    ssm_input,
    ssm_b,
    ssm_c,
    log_decay,
    skip_gain,
    out_proj,
    norm_gain,
    router,
    assignment,
    expert_gate,
    expert_up,
    expert_down,
):
    layer_out, weight_row = layer(
        ssm_input, residual_in, ssm_b, ssm_c, log_decay, skip_gain, norm_gain, router, assignment, out_proj,
        expert_gate[0], expert_up[0], expert_down[0])
    layer_out, weight_row = hand_over(layer_out, weight_row)
    return (layer_out, weight_row[0])


def solution(mesh):
    in_specs = (
        P(("seq", "exp"), None),
        P(("seq", "exp"), None),
        P(("seq", "exp"), None),
        P(("seq", "exp"), None),
        P(("seq", "exp"), None),
        P(),
        P(),
        P(),
        P(),
        P(("seq", "exp"), None),
        P(("seq", "exp"), None, None),
        P(("seq", "exp"), None, None),
        P(("seq", "exp"), None, None),
    )
    out_specs = (P(("seq", "exp"), None), P(("seq", "exp")))
    return jax.shard_map(
        per_device, mesh=mesh, in_specs=in_specs, out_specs=out_specs, check_vma=False
    )
```

```python
import functools

import jax
import jax.numpy as jnp
from jax import lax
from jax.experimental import pallas as pl
from jax.experimental.pallas import tpu as pltpu
from jax.sharding import PartitionSpec as P

SINK_ITERS = 8
LANES = 128
MESH = pl.DeviceIdType.MESH


def place(flat):
    across = lax.axis_size("exp")
    return (flat // across, flat % across)


def own_index():
    return lax.axis_index("seq") * lax.axis_size("exp") + lax.axis_index("exp")


def device_count():
    return lax.axis_size("seq") * lax.axis_size("exp")


def per_lane(columns, group, head_size):
    count = LANES // head_size
    lane = lax.broadcasted_iota(jnp.int32, (1, LANES), 1)
    made = columns[:, group * count:group * count + 1]
    for at in range(1, count):
        head = group * count + at
        made = jnp.where(lane >= at * head_size, columns[:, head:head + 1], made)
    return made


def one_less_exp(y):
    series = 1.0
    for order in range(8, 1, -1):
        series = 1.0 + y / order * series
    return jnp.where(y > -0.5, -y * series, 1.0 - jnp.exp(y))


def layer_kernel(bands, shelves, batch, lag, tail, x_hbm, residual_hbm, b_hbm, c_hbm, decay_hbm, skip_hbm, gain_hbm, router_hbm,
                 chosen_hbm, proj_hbm, gate_hbm, up_hbm, down_hbm, layer_ref, weight_ref,
                 x_ref, residual_ref, b_ref, c_ref, decay_ref, skip_ref, gain_ref, router_ref, chosen_ref,
                 packed_ref, kernel_ref, hot_ref, spread_ref, mixed_ref,
                 states, entry, inner, scanned_out, normed_ref, own_factor,
                 arrived, totals, gathered, scanned, entered, entries, factors, products, spans,
                 out_ref, table_ref, rows_ref, halves, partial, gate, up, down, block,
                 go_send, go_recv, factor_send, factor_recv, up_send, up_recv,
                 span_send, span_recv, down_send, down_recv, back_send, back_recv,
                 row_send, row_recv, pass_send, pass_recv, swap_send, swap_recv, home_send, home_recv,
                 near_send, near_recv, far_send, far_recv, own_sem, load_sem):
    line, spot = lax.axis_index("seq"), lax.axis_index("exp")
    lines = lax.axis_size("seq")
    level, side = spot // 2, spot % 2
    me = own_index()
    devices = device_count()
    slot_of = 2 * line + side
    near = 2 * lines
    levels = lax.axis_size("exp") // 2
    pieces = bands * shelves
    rows, cols = arrived.shape[2:]
    part = rows // levels
    length, width = x_ref.shape
    head_size = width // decay_ref.shape[0]
    lane_groups = width // LANES
    band = width // bands
    band_groups = lane_groups // bands

    def near_place(peer):
        return (peer // 2, 2 * level + peer % 2)

    def far_place(peer):
        return (line, 2 * peer + side)

    def remote(src, dst, send, recv, device):
        return pltpu.make_async_remote_copy(
            src_ref=src, dst_ref=dst, send_sem=send, recv_sem=recv, device_id=device, device_id_type=MESH)

    def region(ref, piece, slot):
        start = pl.multiple_of(piece // shelves * band + slot * cols, cols)
        return ref.at[pl.ds(piece % shelves * rows, rows), pl.ds(start, cols)]

    def go_copy(piece, peer, slot):
        return remote(region(states, piece, peer), arrived.at[piece, slot], go_send.at[piece, peer],
                      go_recv.at[piece, slot], near_place(peer))

    def factor_copy(peer, slot):
        return remote(own_factor.at[peer], factors.at[slot], factor_send.at[peer], factor_recv.at[slot],
                      near_place(peer))

    def up_copy(piece, peer, slot):
        return remote(totals.at[piece, peer], gathered.at[piece, slot], up_send.at[piece, peer],
                      up_recv.at[piece, slot], far_place(peer))

    def span_copy(peer, slot):
        return remote(products, spans.at[slot], span_send.at[peer], span_recv.at[slot], far_place(peer))

    def down_copy(piece, peer, slot):
        return remote(scanned.at[piece, peer], entered.at[piece, slot], down_send.at[piece, peer],
                      down_recv.at[piece, slot], far_place(peer))

    def back_copy(piece, peer, slot):
        return remote(entries.at[piece, peer], region(entry, piece, slot), back_send.at[piece, peer],
                      back_recv.at[piece, slot], near_place(peer))

    barrier = pltpu.get_barrier_semaphore()

    @pl.loop(1, devices)
    def _(step):
        pl.semaphore_signal(
            barrier, inc=1, device_id=place((me + step) % devices), device_id_type=MESH
        )

    proj = halves.at[pl.ds(0, proj_hbm.shape[0])]
    loads = [
        pltpu.make_async_copy(src, dst, load_sem.at[at])
        for at, (src, dst) in enumerate((
            (decay_hbm, decay_ref), (b_hbm, b_ref), (x_hbm, x_ref), (c_hbm, c_ref), (skip_hbm, skip_ref),
            (chosen_hbm, chosen_ref), (gain_hbm, gain_ref), (router_hbm, router_ref), (residual_hbm, residual_ref),
            (proj_hbm, proj), (gate_hbm, gate), (up_hbm, up), (down_hbm, down),
        ))
    ]
    for load in loads:
        load.start()

    before = (lax.broadcasted_iota(jnp.int32, (length, length), 0) <= lax.broadcasted_iota(
        jnp.int32, (length, length), 1)).astype(jnp.float32)
    loads[0].wait()
    decay_row = decay_ref[...]
    sum_row = jnp.dot(decay_row, before, precision=lax.Precision.HIGHEST, preferred_element_type=jnp.float32)
    weight_row = jnp.sqrt(one_less_exp(2.0 * decay_row))
    sums = sum_row.T
    last = sums[length - 1:length]
    tail_weight = jnp.exp(last - sums) * weight_row.T
    factor = jnp.exp(last)
    for group in range(lane_groups):
        at, start = group * LANES // band, group * LANES % band
        own_factor[start // cols, at, :, start % cols:start % cols + LANES] = per_lane(factor, group, head_size)
    factors[slot_of] = own_factor[slot_of]
    for load in loads[1:6]:
        load.wait()

    for at in range(bands):
        for group in range(at * band_groups, (at + 1) * band_groups):
            columns = slice(group * LANES, (group + 1) * LANES)
            tail_in = x_ref[:, columns].astype(jnp.float32) * per_lane(tail_weight, group, head_size)
            made = lax.dot_general(b_ref[...], tail_in.astype(jnp.bfloat16), (((0,), (0,)), ((), ())),
                                   preferred_element_type=jnp.float32)
            states[:, columns] = made.astype(states.dtype)

        if at == 0:
            pl.semaphore_wait(barrier, devices - 1)

            @pl.loop(1, near)
            def _(step):
                factor_copy((slot_of + step) % near, slot_of).start()

        for piece in range(at * shelves, (at + 1) * shelves):
            @pl.loop(1, near)
            def _(step):
                go_copy(piece, (slot_of + step) % near, slot_of).start()

            arrived[piece, slot_of] = region(states, piece, slot_of)[...]

    scores = lax.dot_general(c_ref[...], b_ref[...], (((1,), (1,)), ((), ())), preferred_element_type=jnp.float32)
    causal = lax.broadcasted_iota(jnp.int32, (length, length), 0) >= lax.broadcasted_iota(
        jnp.int32, (length, length), 1)
    scores = jnp.where(causal, scores, 0.0)

    skip = skip_ref[...]

    def inside(first, stop):
        lane = lax.broadcasted_iota(jnp.int32, (1, LANES), 1)
        count = LANES // head_size
        for group in range(first, stop):
            columns = slice(group * LANES, (group + 1) * LANES)
            x = x_ref[:, columns]
            made = None
            for at in range(count):
                head = group * count + at
                distance = sums[:, head:head + 1] - sum_row[head:head + 1]
                mix = jnp.exp(jnp.minimum(distance, 0.0)) * (weight_row[head:head + 1] * scores)
                one = jnp.dot(mix.astype(jnp.bfloat16), x, preferred_element_type=jnp.float32)
                made = one if at == 0 else jnp.where(lane >= at * head_size, one, made)
            inner[:, columns] = made + per_lane(skip, group, head_size) * x.astype(jnp.float32)

    def sorted_rows():
        chosen = chosen_ref[...]
        choices = hot_ref.shape[0]
        capacity = spread_ref.shape[0] // choices
        hot = (lax.broadcasted_iota(jnp.int32, (choices, length), 0) == chosen).astype(jnp.float32)
        hot_ref[...] = hot
        counts = jnp.dot(hot.astype(jnp.bfloat16), before.astype(jnp.bfloat16), preferred_element_type=jnp.float32)
        slot = jnp.sum(counts * hot, axis=0, keepdims=True).astype(jnp.int32) - 1
        position = chosen * capacity + slot
        spread_ref[...] = (lax.broadcasted_iota(jnp.int32, spread_ref.shape, 0) == position).astype(
            jnp.float32).astype(spread_ref.dtype)

    def pair_totals(piece):
        @pl.loop(1, near)
        def _(step):
            peer = (slot_of + near - step) % near
            if piece == 0:
                factor_copy(peer, peer).wait_recv()
            go_copy(piece, peer, peer).wait_recv()

        if piece == 0:
            @pl.loop(0, lines)
            def _(at):
                products[at] = factors[2 * at] * factors[2 * at + 1]

            spans[level] = products[...]

            @pl.loop(1, levels)
            def _(step):
                span_copy((level + step) % levels, level).start()

        @pl.loop(0, lines)
        def _(at):
            both = factors[2 * at + 1, piece // shelves] * arrived[piece, 2 * at].astype(jnp.float32)
            both = both + arrived[piece, 2 * at + 1].astype(jnp.float32)
            totals[piece, :, at] = both.astype(totals.dtype).reshape(levels, part, cols)

        @pl.loop(1, levels)
        def _(step):
            up_copy(piece, (level + step) % levels, level).start()

        gathered[piece, level] = totals[piece, level]

    def pair_entries(piece):
        @pl.loop(1, levels)
        def _(step):
            peer = (level + levels - step) % levels
            if piece == 0:
                span_copy(peer, peer).wait_recv()
            up_copy(piece, peer, peer).wait_recv()

        def advance(k, state):
            at, floor = k // levels, k % levels
            scanned[piece, floor, at] = state.astype(scanned.dtype)
            return spans[floor, at, piece // shelves] * state + gathered[piece, floor, at].astype(jnp.float32)

        lax.fori_loop(0, lines * levels, advance, jnp.zeros((part, cols), jnp.float32))

        @pl.loop(1, levels)
        def _(step):
            down_copy(piece, (level + step) % levels, level).start()

        entered[piece, level] = scanned[piece, level]

    def block_entries(piece):
        @pl.loop(1, levels)
        def _(step):
            peer = (level + levels - step) % levels
            down_copy(piece, peer, peer).wait_recv()

        @pl.loop(0, lines)
        def _(at):
            first = entered[piece, :, at].reshape(rows, cols)
            entries[piece, 2 * at] = first
            second = factors[2 * at, piece // shelves] * first.astype(jnp.float32)
            second = second + arrived[piece, 2 * at].astype(jnp.float32)
            entries[piece, 2 * at + 1] = second.astype(entries.dtype)

        @pl.loop(1, near)
        def _(step):
            back_copy(piece, (slot_of + step) % near, slot_of).start()

        region(entry, piece, slot_of)[...] = entries[piece, slot_of]

    fill = [lane_groups // 2, 3 * lane_groups // 4, lane_groups]
    inside(0, fill[0])
    for step in range(pieces + 2):
        if step < pieces:
            pair_totals(step)
        if 1 <= step <= pieces:
            pair_entries(step - 1)
        if step >= 2:
            block_entries(step - 2)
        if step < 2:
            inside(fill[step], fill[step + 1])
        if step == 2:
            sorted_rows()

    for load in loads[6:10]:
        load.wait()
    grown = jnp.exp(sums)
    chunk = 512
    squares = jnp.zeros((length, 1), jnp.float32)
    for at in range(bands):
        for piece in range(at * shelves, (at + 1) * shelves):
            @pl.loop(1, near)
            def _(step):
                peer = (slot_of + near - step) % near
                back_copy(piece, peer, peer).wait_recv()

        for group in range(at * band_groups, (at + 1) * band_groups):
            columns = slice(group * LANES, (group + 1) * LANES)
            carried = jnp.dot(c_ref[...], entry[:, columns], preferred_element_type=jnp.float32)
            carried = per_lane(grown, group, head_size) * carried
            scanned_out[:, columns] = (inner[:, columns] + carried).astype(scanned_out.dtype)

        depth = slice(at * band, (at + 1) * band)
        for column in range(0, width, chunk):
            columns = slice(column, column + chunk)
            made = jnp.dot(scanned_out[:, depth], proj[depth, columns], preferred_element_type=jnp.float32)
            if at == 0:
                made = made + residual_ref[:, columns].astype(jnp.float32)
            else:
                made = made + mixed_ref[:, columns]
            mixed_ref[:, columns] = made
            if at == bands - 1:
                squares = squares + jnp.sum(made * made, axis=1, keepdims=True)
    scale = lax.rsqrt(squares / width + 1e-05)
    for column in range(0, width, chunk):
        columns = slice(column, column + chunk)
        normed = (mixed_ref[:, columns] * scale * gain_ref[:, columns]).astype(jnp.bfloat16)
        normed_ref[:, columns] = normed
        made = jnp.dot(spread_ref[...], normed, preferred_element_type=jnp.float32)
        packed_ref[:, :, columns] = made.astype(packed_ref.dtype).reshape(*packed_ref.shape[:2], chunk)
    kernel_ref[...] = jnp.exp(lax.dot_general(
        router_ref[...], normed_ref[...], (((1,), (1,)), ((), ())), preferred_element_type=jnp.float32))

    spots = lax.axis_size("exp")
    mine = me // 2
    experts = devices // 2
    partner = me + 1 - 2 * side
    capacity, width = packed_ref.shape[1:]

    def half(at, slot):
        return halves.at[pl.ds(pl.multiple_of((at * experts + slot) * capacity, capacity), capacity)]
    turns = experts // batch

    def row_copy(other, slot):
        return remote(packed_ref.at[other], rows_ref.at[side, slot], row_send.at[other], row_recv.at[slot],
                      place(2 * other + side))

    def pass_copy(at, slot):
        return remote(rows_ref.at[side, slot], rows_ref.at[at, slot], pass_send.at[slot], pass_recv.at[slot],
                      place(partner))

    def swap_copy(slot):
        return remote(half(1 - side, slot), partial.at[slot], swap_send.at[slot], swap_recv.at[slot],
                      place(partner))

    def home_copy(other, slot):
        return remote(half(side, other), out_ref.at[slot], home_send.at[other], home_recv.at[slot],
                      place(2 * other + side))

    def near_copy(other, slot):
        return remote(kernel_ref, table_ref.at[line, slot], near_send.at[other], near_recv.at[slot],
                      (line, other))

    def far_copy(other, slot):
        return remote(table_ref.at[line], table_ref.at[slot], far_send.at[other], far_recv.at[slot],
                      (other, spot))

    own_rows = pltpu.make_async_copy(packed_ref.at[mine], rows_ref.at[side, mine], own_sem.at[0])
    own_table = pltpu.make_async_copy(kernel_ref, table_ref.at[line, spot], own_sem.at[1])
    own_rows.start()
    own_table.start()
    floors = spots // 2
    row, floor = mine // floors, mine % floors

    def target(k):
        return ((row + k % lines) % lines) * floors + (floor + k // lines) % floors

    def source(k):
        return ((row + lines - k % lines) % lines) * floors + (floor + floors - k // lines) % floors

    @pl.loop(1, spots)
    def _(step):
        near_copy((spot + step) % spots, spot).start()

    @pl.loop(1, experts)
    def _(k):
        row_copy(target(k), mine).start()

    own_rows.wait()
    pass_copy(side, mine).start()

    @pl.loop(0, turns + lag + tail)
    def _(turn):
        @pl.when(turn < turns)
        def _():
            @pl.loop(0, batch)
            def _(at):
                k = turn * batch + at

                @pl.when(k > 0)
                def _():
                    row_copy(source(k), source(k)).wait_recv()
                    pass_copy(side, source(k)).start()

        @pl.when(turn == 0)
        def _():
            for load in loads[10:]:
                load.wait()

        @pl.when((turn >= lag) & (turn < turns + lag))
        def _():
            first = (turn - lag) * batch

            @pl.loop(0, batch)
            def _(at):
                pass_copy(1 - side, source(first + at)).wait_recv()

            sources = [source(first + at) for at in range(batch)]
            places = [(k, src, (k * batch + at) * capacity)
                      for k in range(2) for at, src in enumerate(sources)]
            for k, src, start in places:
                block[start:start + capacity] = rows_ref[k, src]
            taken = block[...]
            across = (((1,), (1,)), ((), ()))
            gate_val = lax.dot_general(taken, gate[...], across, preferred_element_type=jnp.float32)
            up_val = lax.dot_general(taken, up[...], across, preferred_element_type=jnp.float32)
            hidden = (gate_val / (1.0 + jnp.exp(-gate_val)) * up_val).astype(jnp.bfloat16)
            piece = 512
            for column in range(0, width, piece):
                made = jnp.dot(hidden, down[:, column:column + piece], preferred_element_type=jnp.float32)
                made = made.astype(halves.dtype)
                for k, src, start in places:
                    half(k, src)[:, column:column + piece] = made[start:start + capacity]

            @pl.loop(0, batch)
            def _(at):
                swap_copy(source(first + at)).start()

        @pl.when(turn >= lag + tail)
        def _():
            @pl.loop(0, batch)
            def _(at):
                k = (turn - lag - tail) * batch + at
                src = source(k)
                swap_copy(src).wait_recv()
                half(side, src)[...] = (
                    half(side, src)[...].astype(jnp.float32) + partial[src].astype(jnp.float32)
                ).astype(halves.dtype)

                @pl.when(k > 0)
                def _():
                    home_copy(src, mine).start()

        @pl.when(turn == turns // 2)
        def _():
            own_table.wait()

            @pl.loop(1, spots)
            def _(step):
                near_copy((spot + step) % spots, (spot + step) % spots).wait_recv()

            @pl.loop(1, lines)
            def _(step):
                far_copy((line + step) % lines, line).start()

    own_out = pltpu.make_async_copy(half(side, mine), out_ref.at[mine], own_sem.at[0])
    own_out.start()

    @pl.loop(1, lines)
    def _(step):
        other = (line + step) % lines
        far_copy(other, other).wait_recv()
        far_copy(other, other).wait_send()

    choices = kernel_ref.shape[0]

    def sweep(_, column):
        def add(at, totals):
            part = table_ref[at]
            row_scale = 1.0 / jnp.sum(part * column[None], axis=1, keepdims=True)
            return totals + jnp.sum(part * row_scale, axis=0)

        totals = lax.fori_loop(0, lines, add, jnp.zeros((choices, length), jnp.float32))
        return 1.0 / jnp.sum(totals, axis=1, keepdims=True)

    column = lax.fori_loop(0, SINK_ITERS, sweep, jnp.ones((choices, 1), jnp.float32))
    weighted = kernel_ref[...] * column
    picked = jnp.sum(jnp.where(hot_ref[...] > 0.0, weighted, 0.0), axis=0, keepdims=True)
    weight = choices * picked / jnp.sum(weighted, axis=0, keepdims=True)
    weight_ref[...] = weight
    same = lax.broadcasted_iota(jnp.int32, (length, length), 0) == lax.broadcasted_iota(
        jnp.int32, (length, length), 1)
    weight_column = jnp.sum(jnp.where(same, weight, 0.0), axis=1, keepdims=True)

    @pl.loop(1, spots)
    def _(step):
        near_copy((spot + step) % spots, spot).wait_send()

    @pl.loop(0, experts)
    def _(step):
        pass_copy(side, step).wait_send()
        swap_copy(step).wait_send()

    @pl.loop(1, experts)
    def _(step):
        other = (mine + step) % experts
        row_copy(other, other).wait_send()
        home_copy(other, other).wait_recv()
        home_copy(other, other).wait_send()

    own_out.wait()
    for column in range(0, width, 512):
        columns = slice(column, column + 512)
        made = lax.dot_general(spread_ref[...], out_ref[:, :, columns].reshape(experts * capacity, 512),
                               (((0,), (0,)), ((), ())), preferred_element_type=jnp.float32)
        layer_ref[:, columns] = (mixed_ref[:, columns] + weight_column * made).astype(layer_ref.dtype)

    @pl.loop(1, near)
    def _(step):
        peer = (slot_of + near - step) % near
        factor_copy(peer, peer).wait_send()
        for piece in range(pieces):
            go_copy(piece, peer, peer).wait_send()
            back_copy(piece, peer, peer).wait_send()

    @pl.loop(1, levels)
    def _(step):
        peer = (level + levels - step) % levels
        span_copy(peer, peer).wait_send()
        for piece in range(pieces):
            up_copy(piece, peer, peer).wait_send()
            down_copy(piece, peer, peer).wait_send()


def layer(x, residual, b, c, decay, skip, gain, router, assignment, proj, gate_half, up_half, down_half):
    devices = device_count()
    lines, spots = lax.axis_size("seq"), lax.axis_size("exp")
    levels, near, experts = spots // 2, 2 * lines, devices // 2
    length, width = x.shape
    state_size = b.shape[1]
    choices = router.shape[1]
    model_width = proj.shape[1]
    hidden_units = down_half.shape[0]
    capacity = max(16, 2 * length // choices)
    bands = max(1, min(2, width // (near * LANES)))
    shelves = max(1, min(1, state_size // (16 * levels)))
    pieces = bands * shelves
    rows, cols = state_size // shelves, width // (near * bands)
    part = rows // levels
    group, lag, tail = 1, 3, 2
    dma = pltpu.SemaphoreType.DMA
    vmem = pl.BlockSpec(memory_space=pltpu.VMEM)

    def half_words(*shape):
        return pltpu.VMEM(shape, jnp.bfloat16)

    def words(*shape):
        return pltpu.VMEM(shape, jnp.float32)

    flat = half_words(pieces, near, rows, cols)
    deep = half_words(pieces, levels, lines, part, cols)
    single = half_words(experts, capacity, model_width)
    weights = half_words(hidden_units, model_width)
    nears, fars, each = dma((pieces, near)), dma((pieces, levels)), dma((experts,))
    heads = decay.shape[1]
    return pl.pallas_call(
        functools.partial(layer_kernel, bands, shelves, group, lag, tail),
        out_shape=(
            jax.ShapeDtypeStruct((length, model_width), jnp.bfloat16),
            jax.ShapeDtypeStruct((1, length), jnp.float32),
        ),
        in_specs=[pl.BlockSpec(memory_space=pl.ANY)] * 13,
        out_specs=(vmem, vmem),
        scratch_shapes=[
            half_words(length, width), half_words(length, model_width), half_words(length, state_size),
            half_words(length, state_size), words(heads, length), words(1, heads), words(1, model_width),
            half_words(choices, model_width), pltpu.VMEM((1, length), jnp.int32),
            single, words(choices, length), words(choices, length), half_words(choices * capacity, length),
            words(length, model_width),
            half_words(state_size, width), half_words(state_size, width), words(length, width),
            half_words(length, width), half_words(length, model_width), words(near, bands, 1, cols),
            flat, deep, deep, deep, deep, flat, words(near, bands, 1, cols),
            words(lines, bands, 1, cols), words(levels, lines, bands, 1, cols),
            single, words(lines, spots, choices, length), half_words(2, experts, capacity, model_width),
            half_words(max(2 * experts * capacity, width), model_width), single, weights, weights, weights,
            half_words(2 * group * capacity, model_width),
            nears, nears, dma((near,)), dma((near,)), fars, fars,
            dma((levels,)), dma((levels,)), fars, fars, nears, nears,
            each, each, each, each, each, each, each, each,
            dma((spots,)), dma((spots,)), dma((lines,)), dma((lines,)), dma((2,)), dma((13,)),
        ],
        compiler_params=pltpu.CompilerParams(
            collective_id=0, has_side_effects=True, vmem_limit_bytes=60 << 20
        ),
        name="layer",
    )(x, residual, b, c, decay.T, skip[None, :], gain[None, :], router.T, assignment.T, proj,
      gate_half.T, up_half.T, down_half)


def hand_over_kernel(layer_ref, weight_ref, layer_out, weight_out):
    layer_out[...] = layer_ref[...]
    weight_out[...] = weight_ref[...]


def hand_over(layer_out, weight):
    vmem = pl.BlockSpec(memory_space=pltpu.VMEM)
    return pl.pallas_call(
        hand_over_kernel,
        out_shape=(
            jax.ShapeDtypeStruct(layer_out.shape, layer_out.dtype),
            jax.ShapeDtypeStruct(weight.shape, weight.dtype),
        ),
        in_specs=[vmem, vmem],
        out_specs=(vmem, vmem),
        name="hand_over",
    )(layer_out, weight)


def per_device(
    residual_in,
    ssm_input,
    ssm_b,
    ssm_c,
    log_decay,
    skip_gain,
    out_proj,
    norm_gain,
    router,
    assignment,
    expert_gate,
    expert_up,
    expert_down,
):
    layer_out, weight_row = layer(
        ssm_input, residual_in, ssm_b, ssm_c, log_decay, skip_gain, norm_gain, router, assignment, out_proj,
        expert_gate[0], expert_up[0], expert_down[0])
    layer_out, weight_row = hand_over(layer_out, weight_row)
    return (layer_out, weight_row[0])


def solution(mesh):
    in_specs = (
        P(("seq", "exp"), None),
        P(("seq", "exp"), None),
        P(("seq", "exp"), None),
        P(("seq", "exp"), None),
        P(("seq", "exp"), None),
        P(),
        P(),
        P(),
        P(),
        P(("seq", "exp"), None),
        P(("seq", "exp"), None, None),
        P(("seq", "exp"), None, None),
        P(("seq", "exp"), None, None),
    )
    out_specs = (P(("seq", "exp"), None), P(("seq", "exp")))
    return jax.shard_map(
        per_device, mesh=mesh, in_specs=in_specs, out_specs=out_specs, check_vma=False
    )
```

```python
import functools

import jax
import jax.numpy as jnp
from jax import lax
from jax.experimental import pallas as pl
from jax.experimental.pallas import tpu as pltpu
from jax.sharding import PartitionSpec as P

SINK_ITERS = 8
LANES = 128
MESH = pl.DeviceIdType.MESH


def place(flat):
    across = lax.axis_size("exp")
    return (flat // across, flat % across)


def own_index():
    return lax.axis_index("seq") * lax.axis_size("exp") + lax.axis_index("exp")


def device_count():
    return lax.axis_size("seq") * lax.axis_size("exp")


def per_lane(columns, group, head_size):
    count = LANES // head_size
    lane = lax.broadcasted_iota(jnp.int32, (1, LANES), 1)
    made = columns[:, group * count:group * count + 1]
    for at in range(1, count):
        head = group * count + at
        made = jnp.where(lane >= at * head_size, columns[:, head:head + 1], made)
    return made


def one_less_exp(y):
    series = 1.0
    for order in range(8, 1, -1):
        series = 1.0 + y / order * series
    return jnp.where(y > -0.5, -y * series, 1.0 - jnp.exp(y))


def layer_kernel(bands, shelves, batch, lag, tail, x_hbm, residual_hbm, b_hbm, c_hbm, decay_hbm, skip_hbm, gain_hbm, router_hbm,
                 chosen_hbm, proj_hbm, gate_hbm, up_hbm, down_hbm, layer_ref, weight_ref,
                 x_ref, residual_ref, b_ref, c_ref, decay_ref, skip_ref, gain_ref, router_ref, chosen_ref,
                 packed_ref, kernel_ref, hot_ref, spread_ref, mixed_ref,
                 states, entry, inner, scanned_out, normed_ref, own_factor,
                 arrived, totals, gathered, scanned, entered, entries, factors, products, spans,
                 out_ref, table_ref, rows_ref, halves, partial, gate, up, down, block,
                 go_send, go_recv, factor_send, factor_recv, up_send, up_recv,
                 span_send, span_recv, down_send, down_recv, back_send, back_recv,
                 row_send, row_recv, pass_send, pass_recv, swap_send, swap_recv, home_send, home_recv,
                 near_send, near_recv, far_send, far_recv, own_sem, load_sem):
    line, spot = lax.axis_index("seq"), lax.axis_index("exp")
    lines = lax.axis_size("seq")
    level, side = spot // 2, spot % 2
    me = own_index()
    devices = device_count()
    slot_of = 2 * line + side
    near = 2 * lines
    levels = lax.axis_size("exp") // 2
    pieces = bands * shelves
    rows, cols = arrived.shape[2:]
    part = rows // levels
    length, width = x_ref.shape
    head_size = width // decay_ref.shape[0]
    lane_groups = width // LANES
    band = width // bands
    band_groups = lane_groups // bands

    def near_place(peer):
        return (peer // 2, 2 * level + peer % 2)

    def far_place(peer):
        return (line, 2 * peer + side)

    def remote(src, dst, send, recv, device):
        return pltpu.make_async_remote_copy(
            src_ref=src, dst_ref=dst, send_sem=send, recv_sem=recv, device_id=device, device_id_type=MESH)

    def region(ref, piece, slot):
        start = pl.multiple_of(piece // shelves * band + slot * cols, cols)
        return ref.at[pl.ds(piece % shelves * rows, rows), pl.ds(start, cols)]

    def go_copy(piece, peer, slot):
        return remote(region(states, piece, peer), arrived.at[piece, slot], go_send.at[piece, peer],
                      go_recv.at[piece, slot], near_place(peer))

    def factor_copy(peer, slot):
        return remote(own_factor.at[peer], factors.at[slot], factor_send.at[peer], factor_recv.at[slot],
                      near_place(peer))

    def up_copy(piece, peer, slot):
        return remote(totals.at[piece, peer], gathered.at[piece, slot], up_send.at[piece, peer],
                      up_recv.at[piece, slot], far_place(peer))

    def span_copy(peer, slot):
        return remote(products, spans.at[slot], span_send.at[peer], span_recv.at[slot], far_place(peer))

    def down_copy(piece, peer, slot):
        return remote(scanned.at[piece, peer], entered.at[piece, slot], down_send.at[piece, peer],
                      down_recv.at[piece, slot], far_place(peer))

    def back_copy(piece, peer, slot):
        return remote(entries.at[piece, peer], region(entry, piece, slot), back_send.at[piece, peer],
                      back_recv.at[piece, slot], near_place(peer))

    barrier = pltpu.get_barrier_semaphore()

    @pl.loop(1, devices)
    def _(step):
        pl.semaphore_signal(
            barrier, inc=1, device_id=place((me + step) % devices), device_id_type=MESH
        )

    proj = halves.at[pl.ds(0, proj_hbm.shape[0])]
    loads = [
        pltpu.make_async_copy(src, dst, load_sem.at[at])
        for at, (src, dst) in enumerate((
            (decay_hbm, decay_ref), (b_hbm, b_ref), (x_hbm, x_ref), (c_hbm, c_ref), (skip_hbm, skip_ref),
            (chosen_hbm, chosen_ref), (gain_hbm, gain_ref), (router_hbm, router_ref), (residual_hbm, residual_ref),
            (proj_hbm, proj), (gate_hbm, gate), (up_hbm, up), (down_hbm, down),
        ))
    ]
    for load in loads[:9]:
        load.start()

    before = (lax.broadcasted_iota(jnp.int32, (length, length), 0) <= lax.broadcasted_iota(
        jnp.int32, (length, length), 1)).astype(jnp.float32)
    loads[0].wait()
    decay_row = decay_ref[...]
    sum_row = jnp.dot(decay_row, before, precision=lax.Precision.HIGHEST, preferred_element_type=jnp.float32)
    weight_row = jnp.sqrt(one_less_exp(2.0 * decay_row))
    sums = sum_row.T
    last = sums[length - 1:length]
    tail_weight = jnp.exp(last - sums) * weight_row.T
    factor = jnp.exp(last)
    for group in range(lane_groups):
        at, start = group * LANES // band, group * LANES % band
        own_factor[start // cols, at, :, start % cols:start % cols + LANES] = per_lane(factor, group, head_size)
    factors[slot_of] = own_factor[slot_of]
    for load in loads[1:6]:
        load.wait()

    for at in range(bands):
        for group in range(at * band_groups, (at + 1) * band_groups):
            columns = slice(group * LANES, (group + 1) * LANES)
            tail_in = x_ref[:, columns].astype(jnp.float32) * per_lane(tail_weight, group, head_size)
            made = lax.dot_general(b_ref[...], tail_in.astype(jnp.bfloat16), (((0,), (0,)), ((), ())),
                                   preferred_element_type=jnp.float32)
            states[:, columns] = made.astype(states.dtype)

        if at == 0:
            pl.semaphore_wait(barrier, devices - 1)

            @pl.loop(1, near)
            def _(step):
                factor_copy((slot_of + step) % near, slot_of).start()

        for piece in range(at * shelves, (at + 1) * shelves):
            @pl.loop(1, near)
            def _(step):
                go_copy(piece, (slot_of + step) % near, slot_of).start()

            arrived[piece, slot_of] = region(states, piece, slot_of)[...]

    loads[9].start()
    scores = lax.dot_general(c_ref[...], b_ref[...], (((1,), (1,)), ((), ())), preferred_element_type=jnp.float32)
    causal = lax.broadcasted_iota(jnp.int32, (length, length), 0) >= lax.broadcasted_iota(
        jnp.int32, (length, length), 1)
    scores = jnp.where(causal, scores, 0.0)

    skip = skip_ref[...]

    def inside(first, stop):
        lane = lax.broadcasted_iota(jnp.int32, (1, LANES), 1)
        count = LANES // head_size
        for group in range(first, stop):
            columns = slice(group * LANES, (group + 1) * LANES)
            x = x_ref[:, columns]
            made = None
            for at in range(count):
                head = group * count + at
                distance = sums[:, head:head + 1] - sum_row[head:head + 1]
                mix = jnp.exp(jnp.minimum(distance, 0.0)) * (weight_row[head:head + 1] * scores)
                one = jnp.dot(mix.astype(jnp.bfloat16), x, preferred_element_type=jnp.float32)
                made = one if at == 0 else jnp.where(lane >= at * head_size, one, made)
            inner[:, columns] = made + per_lane(skip, group, head_size) * x.astype(jnp.float32)

    def sorted_rows():
        chosen = chosen_ref[...]
        choices = hot_ref.shape[0]
        capacity = spread_ref.shape[0] // choices
        hot = (lax.broadcasted_iota(jnp.int32, (choices, length), 0) == chosen).astype(jnp.float32)
        hot_ref[...] = hot
        counts = jnp.dot(hot.astype(jnp.bfloat16), before.astype(jnp.bfloat16), preferred_element_type=jnp.float32)
        slot = jnp.sum(counts * hot, axis=0, keepdims=True).astype(jnp.int32) - 1
        position = chosen * capacity + slot
        spread_ref[...] = (lax.broadcasted_iota(jnp.int32, spread_ref.shape, 0) == position).astype(
            jnp.float32).astype(spread_ref.dtype)

    def pair_totals(piece):
        @pl.loop(1, near)
        def _(step):
            peer = (slot_of + near - step) % near
            if piece == 0:
                factor_copy(peer, peer).wait_recv()
            go_copy(piece, peer, peer).wait_recv()

        if piece == 0:
            @pl.loop(0, lines)
            def _(at):
                products[at] = factors[2 * at] * factors[2 * at + 1]

            spans[level] = products[...]

            @pl.loop(1, levels)
            def _(step):
                span_copy((level + step) % levels, level).start()

        @pl.loop(0, lines)
        def _(at):
            both = factors[2 * at + 1, piece // shelves] * arrived[piece, 2 * at].astype(jnp.float32)
            both = both + arrived[piece, 2 * at + 1].astype(jnp.float32)
            totals[piece, :, at] = both.astype(totals.dtype).reshape(levels, part, cols)

        @pl.loop(1, levels)
        def _(step):
            up_copy(piece, (level + step) % levels, level).start()

        gathered[piece, level] = totals[piece, level]

    def pair_entries(piece):
        @pl.loop(1, levels)
        def _(step):
            peer = (level + levels - step) % levels
            if piece == 0:
                span_copy(peer, peer).wait_recv()
            up_copy(piece, peer, peer).wait_recv()

        def advance(k, state):
            at, floor = k // levels, k % levels
            scanned[piece, floor, at] = state.astype(scanned.dtype)
            return spans[floor, at, piece // shelves] * state + gathered[piece, floor, at].astype(jnp.float32)

        lax.fori_loop(0, lines * levels, advance, jnp.zeros((part, cols), jnp.float32))

        @pl.loop(1, levels)
        def _(step):
            down_copy(piece, (level + step) % levels, level).start()

        entered[piece, level] = scanned[piece, level]

    def block_entries(piece):
        @pl.loop(1, levels)
        def _(step):
            peer = (level + levels - step) % levels
            down_copy(piece, peer, peer).wait_recv()

        @pl.loop(0, lines)
        def _(at):
            first = entered[piece, :, at].reshape(rows, cols)
            entries[piece, 2 * at] = first
            second = factors[2 * at, piece // shelves] * first.astype(jnp.float32)
            second = second + arrived[piece, 2 * at].astype(jnp.float32)
            entries[piece, 2 * at + 1] = second.astype(entries.dtype)

        @pl.loop(1, near)
        def _(step):
            back_copy(piece, (slot_of + step) % near, slot_of).start()

        region(entry, piece, slot_of)[...] = entries[piece, slot_of]

    fill = [lane_groups // 2, 3 * lane_groups // 4, lane_groups]
    inside(0, fill[0])
    for step in range(pieces + 2):
        if step < pieces:
            pair_totals(step)
        if 1 <= step <= pieces:
            pair_entries(step - 1)
        if step >= 2:
            block_entries(step - 2)
        if step < 2:
            inside(fill[step], fill[step + 1])
        if step == 2:
            sorted_rows()

    for load in loads[6:10]:
        load.wait()
    grown = jnp.exp(sums)
    chunk = 512
    squares = jnp.zeros((length, 1), jnp.float32)
    for at in range(bands):
        for piece in range(at * shelves, (at + 1) * shelves):
            @pl.loop(1, near)
            def _(step):
                peer = (slot_of + near - step) % near
                back_copy(piece, peer, peer).wait_recv()

        for group in range(at * band_groups, (at + 1) * band_groups):
            columns = slice(group * LANES, (group + 1) * LANES)
            carried = jnp.dot(c_ref[...], entry[:, columns], preferred_element_type=jnp.float32)
            carried = per_lane(grown, group, head_size) * carried
            scanned_out[:, columns] = (inner[:, columns] + carried).astype(scanned_out.dtype)

        depth = slice(at * band, (at + 1) * band)
        for column in range(0, width, chunk):
            columns = slice(column, column + chunk)
            made = jnp.dot(scanned_out[:, depth], proj[depth, columns], preferred_element_type=jnp.float32)
            if at == 0:
                made = made + residual_ref[:, columns].astype(jnp.float32)
            else:
                made = made + mixed_ref[:, columns]
            mixed_ref[:, columns] = made
            if at == bands - 1:
                squares = squares + jnp.sum(made * made, axis=1, keepdims=True)
    scale = lax.rsqrt(squares / width + 1e-05)
    for column in range(0, width, chunk):
        columns = slice(column, column + chunk)
        normed = (mixed_ref[:, columns] * scale * gain_ref[:, columns]).astype(jnp.bfloat16)
        normed_ref[:, columns] = normed
        made = jnp.dot(spread_ref[...], normed, preferred_element_type=jnp.float32)
        packed_ref[:, :, columns] = made.astype(packed_ref.dtype).reshape(*packed_ref.shape[:2], chunk)
    kernel_ref[...] = jnp.exp(lax.dot_general(
        router_ref[...], normed_ref[...], (((1,), (1,)), ((), ())), preferred_element_type=jnp.float32))

    for load in loads[10:]:
        load.start()
    spots = lax.axis_size("exp")
    mine = me // 2
    experts = devices // 2
    partner = me + 1 - 2 * side
    capacity, width = packed_ref.shape[1:]

    def half(at, slot):
        return halves.at[pl.ds(pl.multiple_of((at * experts + slot) * capacity, capacity), capacity)]
    turns = experts // batch

    def row_copy(other, slot):
        return remote(packed_ref.at[other], rows_ref.at[side, slot], row_send.at[other], row_recv.at[slot],
                      place(2 * other + side))

    def pass_copy(at, slot):
        return remote(rows_ref.at[side, slot], rows_ref.at[at, slot], pass_send.at[slot], pass_recv.at[slot],
                      place(partner))

    def swap_copy(slot):
        return remote(half(1 - side, slot), partial.at[slot], swap_send.at[slot], swap_recv.at[slot],
                      place(partner))

    def home_copy(other, slot):
        return remote(half(side, other), out_ref.at[slot], home_send.at[other], home_recv.at[slot],
                      place(2 * other + side))

    def near_copy(other, slot):
        return remote(kernel_ref, table_ref.at[line, slot], near_send.at[other], near_recv.at[slot],
                      (line, other))

    def far_copy(other, slot):
        return remote(table_ref.at[line], table_ref.at[slot], far_send.at[other], far_recv.at[slot],
                      (other, spot))

    own_rows = pltpu.make_async_copy(packed_ref.at[mine], rows_ref.at[side, mine], own_sem.at[0])
    own_table = pltpu.make_async_copy(kernel_ref, table_ref.at[line, spot], own_sem.at[1])
    own_rows.start()
    own_table.start()
    floors = spots // 2
    row, floor = mine // floors, mine % floors

    def target(k):
        return ((row + k % lines) % lines) * floors + (floor + k // lines) % floors

    def source(k):
        return ((row + lines - k % lines) % lines) * floors + (floor + floors - k // lines) % floors

    @pl.loop(1, spots)
    def _(step):
        near_copy((spot + step) % spots, spot).start()

    @pl.loop(1, experts)
    def _(k):
        row_copy(target(k), mine).start()

    own_rows.wait()
    pass_copy(side, mine).start()

    @pl.loop(0, turns + lag + tail)
    def _(turn):
        @pl.when(turn < turns)
        def _():
            @pl.loop(0, batch)
            def _(at):
                k = turn * batch + at

                @pl.when(k > 0)
                def _():
                    row_copy(source(k), source(k)).wait_recv()
                    pass_copy(side, source(k)).start()

        @pl.when(turn == 0)
        def _():
            for load in loads[10:]:
                load.wait()

        @pl.when((turn >= lag) & (turn < turns + lag))
        def _():
            first = (turn - lag) * batch

            @pl.loop(0, batch)
            def _(at):
                pass_copy(1 - side, source(first + at)).wait_recv()

            sources = [source(first + at) for at in range(batch)]
            places = [(k, src, (k * batch + at) * capacity)
                      for k in range(2) for at, src in enumerate(sources)]
            for k, src, start in places:
                block[start:start + capacity] = rows_ref[k, src]
            taken = block[...]
            across = (((1,), (1,)), ((), ()))
            gate_val = lax.dot_general(taken, gate[...], across, preferred_element_type=jnp.float32)
            up_val = lax.dot_general(taken, up[...], across, preferred_element_type=jnp.float32)
            hidden = (gate_val / (1.0 + jnp.exp(-gate_val)) * up_val).astype(jnp.bfloat16)
            piece = 512
            for column in range(0, width, piece):
                made = jnp.dot(hidden, down[:, column:column + piece], preferred_element_type=jnp.float32)
                made = made.astype(halves.dtype)
                for k, src, start in places:
                    half(k, src)[:, column:column + piece] = made[start:start + capacity]

            @pl.loop(0, batch)
            def _(at):
                swap_copy(source(first + at)).start()

        @pl.when(turn >= lag + tail)
        def _():
            @pl.loop(0, batch)
            def _(at):
                k = (turn - lag - tail) * batch + at
                src = source(k)
                swap_copy(src).wait_recv()
                half(side, src)[...] = (
                    half(side, src)[...].astype(jnp.float32) + partial[src].astype(jnp.float32)
                ).astype(halves.dtype)

                @pl.when(k > 0)
                def _():
                    home_copy(src, mine).start()

        @pl.when(turn == turns // 2)
        def _():
            own_table.wait()

            @pl.loop(1, spots)
            def _(step):
                near_copy((spot + step) % spots, (spot + step) % spots).wait_recv()

            @pl.loop(1, lines)
            def _(step):
                far_copy((line + step) % lines, line).start()

    own_out = pltpu.make_async_copy(half(side, mine), out_ref.at[mine], own_sem.at[0])
    own_out.start()

    @pl.loop(1, lines)
    def _(step):
        other = (line + step) % lines
        far_copy(other, other).wait_recv()
        far_copy(other, other).wait_send()

    choices = kernel_ref.shape[0]

    def sweep(_, column):
        def add(at, totals):
            part = table_ref[at]
            row_scale = 1.0 / jnp.sum(part * column[None], axis=1, keepdims=True)
            return totals + jnp.sum(part * row_scale, axis=0)

        totals = lax.fori_loop(0, lines, add, jnp.zeros((choices, length), jnp.float32))
        return 1.0 / jnp.sum(totals, axis=1, keepdims=True)

    column = lax.fori_loop(0, SINK_ITERS, sweep, jnp.ones((choices, 1), jnp.float32))
    weighted = kernel_ref[...] * column
    picked = jnp.sum(jnp.where(hot_ref[...] > 0.0, weighted, 0.0), axis=0, keepdims=True)
    weight = choices * picked / jnp.sum(weighted, axis=0, keepdims=True)
    weight_ref[...] = weight
    same = lax.broadcasted_iota(jnp.int32, (length, length), 0) == lax.broadcasted_iota(
        jnp.int32, (length, length), 1)
    weight_column = jnp.sum(jnp.where(same, weight, 0.0), axis=1, keepdims=True)

    @pl.loop(1, spots)
    def _(step):
        near_copy((spot + step) % spots, spot).wait_send()

    @pl.loop(0, experts)
    def _(step):
        pass_copy(side, step).wait_send()
        swap_copy(step).wait_send()

    @pl.loop(1, experts)
    def _(step):
        other = (mine + step) % experts
        row_copy(other, other).wait_send()
        home_copy(other, other).wait_recv()
        home_copy(other, other).wait_send()

    own_out.wait()
    for column in range(0, width, 512):
        columns = slice(column, column + 512)
        made = lax.dot_general(spread_ref[...], out_ref[:, :, columns].reshape(experts * capacity, 512),
                               (((0,), (0,)), ((), ())), preferred_element_type=jnp.float32)
        layer_ref[:, columns] = (mixed_ref[:, columns] + weight_column * made).astype(layer_ref.dtype)

    @pl.loop(1, near)
    def _(step):
        peer = (slot_of + near - step) % near
        factor_copy(peer, peer).wait_send()
        for piece in range(pieces):
            go_copy(piece, peer, peer).wait_send()
            back_copy(piece, peer, peer).wait_send()

    @pl.loop(1, levels)
    def _(step):
        peer = (level + levels - step) % levels
        span_copy(peer, peer).wait_send()
        for piece in range(pieces):
            up_copy(piece, peer, peer).wait_send()
            down_copy(piece, peer, peer).wait_send()


def layer(x, residual, b, c, decay, skip, gain, router, assignment, proj, gate_half, up_half, down_half):
    devices = device_count()
    lines, spots = lax.axis_size("seq"), lax.axis_size("exp")
    levels, near, experts = spots // 2, 2 * lines, devices // 2
    length, width = x.shape
    state_size = b.shape[1]
    choices = router.shape[1]
    model_width = proj.shape[1]
    hidden_units = down_half.shape[0]
    capacity = max(16, 2 * length // choices)
    bands = max(1, min(2, width // (near * LANES)))
    shelves = max(1, min(1, state_size // (16 * levels)))
    pieces = bands * shelves
    rows, cols = state_size // shelves, width // (near * bands)
    part = rows // levels
    group, lag, tail = 1, 3, 2
    dma = pltpu.SemaphoreType.DMA
    vmem = pl.BlockSpec(memory_space=pltpu.VMEM)

    def half_words(*shape):
        return pltpu.VMEM(shape, jnp.bfloat16)

    def words(*shape):
        return pltpu.VMEM(shape, jnp.float32)

    flat = half_words(pieces, near, rows, cols)
    deep = half_words(pieces, levels, lines, part, cols)
    single = half_words(experts, capacity, model_width)
    weights = half_words(hidden_units, model_width)
    nears, fars, each = dma((pieces, near)), dma((pieces, levels)), dma((experts,))
    heads = decay.shape[1]
    return pl.pallas_call(
        functools.partial(layer_kernel, bands, shelves, group, lag, tail),
        out_shape=(
            jax.ShapeDtypeStruct((length, model_width), jnp.bfloat16),
            jax.ShapeDtypeStruct((1, length), jnp.float32),
        ),
        in_specs=[pl.BlockSpec(memory_space=pl.ANY)] * 13,
        out_specs=(vmem, vmem),
        scratch_shapes=[
            half_words(length, width), half_words(length, model_width), half_words(length, state_size),
            half_words(length, state_size), words(heads, length), words(1, heads), words(1, model_width),
            half_words(choices, model_width), pltpu.VMEM((1, length), jnp.int32),
            single, words(choices, length), words(choices, length), half_words(choices * capacity, length),
            words(length, model_width),
            half_words(state_size, width), half_words(state_size, width), words(length, width),
            half_words(length, width), half_words(length, model_width), words(near, bands, 1, cols),
            flat, deep, deep, deep, deep, flat, words(near, bands, 1, cols),
            words(lines, bands, 1, cols), words(levels, lines, bands, 1, cols),
            single, words(lines, spots, choices, length), half_words(2, experts, capacity, model_width),
            half_words(max(2 * experts * capacity, width), model_width), single, weights, weights, weights,
            half_words(2 * group * capacity, model_width),
            nears, nears, dma((near,)), dma((near,)), fars, fars,
            dma((levels,)), dma((levels,)), fars, fars, nears, nears,
            each, each, each, each, each, each, each, each,
            dma((spots,)), dma((spots,)), dma((lines,)), dma((lines,)), dma((2,)), dma((13,)),
        ],
        compiler_params=pltpu.CompilerParams(
            collective_id=0, has_side_effects=True, vmem_limit_bytes=60 << 20
        ),
        name="layer",
    )(x, residual, b, c, decay.T, skip[None, :], gain[None, :], router.T, assignment.T, proj,
      gate_half.T, up_half.T, down_half)


def hand_over_kernel(layer_ref, weight_ref, layer_out, weight_out):
    layer_out[...] = layer_ref[...]
    weight_out[...] = weight_ref[...]


def hand_over(layer_out, weight):
    vmem = pl.BlockSpec(memory_space=pltpu.VMEM)
    return pl.pallas_call(
        hand_over_kernel,
        out_shape=(
            jax.ShapeDtypeStruct(layer_out.shape, layer_out.dtype),
            jax.ShapeDtypeStruct(weight.shape, weight.dtype),
        ),
        in_specs=[vmem, vmem],
        out_specs=(vmem, vmem),
        name="hand_over",
    )(layer_out, weight)


def per_device(
    residual_in,
    ssm_input,
    ssm_b,
    ssm_c,
    log_decay,
    skip_gain,
    out_proj,
    norm_gain,
    router,
    assignment,
    expert_gate,
    expert_up,
    expert_down,
):
    layer_out, weight_row = layer(
        ssm_input, residual_in, ssm_b, ssm_c, log_decay, skip_gain, norm_gain, router, assignment, out_proj,
        expert_gate[0], expert_up[0], expert_down[0])
    layer_out, weight_row = hand_over(layer_out, weight_row)
    return (layer_out, weight_row[0])


def solution(mesh):
    in_specs = (
        P(("seq", "exp"), None),
        P(("seq", "exp"), None),
        P(("seq", "exp"), None),
        P(("seq", "exp"), None),
        P(("seq", "exp"), None),
        P(),
        P(),
        P(),
        P(),
        P(("seq", "exp"), None),
        P(("seq", "exp"), None, None),
        P(("seq", "exp"), None, None),
        P(("seq", "exp"), None, None),
    )
    out_specs = (P(("seq", "exp"), None), P(("seq", "exp")))
    return jax.shard_map(
        per_device, mesh=mesh, in_specs=in_specs, out_specs=out_specs, check_vma=False
    )
```

```python
import functools

import jax
import jax.numpy as jnp
from jax import lax
from jax.experimental import pallas as pl
from jax.experimental.pallas import tpu as pltpu
from jax.sharding import PartitionSpec as P

SINK_ITERS = 8
LANES = 128
MESH = pl.DeviceIdType.MESH


def place(flat):
    across = lax.axis_size("exp")
    return (flat // across, flat % across)


def own_index():
    return lax.axis_index("seq") * lax.axis_size("exp") + lax.axis_index("exp")


def device_count():
    return lax.axis_size("seq") * lax.axis_size("exp")


def per_lane(columns, group, head_size):
    count = LANES // head_size
    lane = lax.broadcasted_iota(jnp.int32, (1, LANES), 1)
    made = columns[:, group * count:group * count + 1]
    for at in range(1, count):
        head = group * count + at
        made = jnp.where(lane >= at * head_size, columns[:, head:head + 1], made)
    return made


def one_less_exp(y):
    series = 1.0
    for order in range(8, 1, -1):
        series = 1.0 + y / order * series
    return jnp.where(y > -0.5, -y * series, 1.0 - jnp.exp(y))


def layer_kernel(bands, shelves, batch, lag, tail, x_hbm, residual_hbm, b_hbm, c_hbm, decay_hbm, skip_hbm, gain_hbm, router_hbm,
                 chosen_hbm, proj_hbm, gate_hbm, up_hbm, down_hbm, layer_ref, weight_ref,
                 x_ref, residual_ref, b_ref, c_ref, decay_ref, skip_ref, gain_ref, router_ref, chosen_ref,
                 packed_ref, kernel_ref, hot_ref, spread_ref, mixed_ref,
                 states, entry, inner, scanned_out, normed_ref, own_factor,
                 arrived, totals, gathered, scanned, entered, entries, factors, products, spans,
                 out_ref, table_ref, rows_ref, halves, partial, gate, up, down, block,
                 go_send, go_recv, factor_send, factor_recv, up_send, up_recv,
                 span_send, span_recv, down_send, down_recv, back_send, back_recv,
                 row_send, row_recv, pass_send, pass_recv, swap_send, swap_recv, home_send, home_recv,
                 near_send, near_recv, far_send, far_recv, own_sem, load_sem):
    line, spot = lax.axis_index("seq"), lax.axis_index("exp")
    lines = lax.axis_size("seq")
    level, side = spot // 2, spot % 2
    me = own_index()
    devices = device_count()
    slot_of = 2 * line + side
    near = 2 * lines
    levels = lax.axis_size("exp") // 2
    pieces = bands * shelves
    rows, cols = arrived.shape[2:]
    part = rows // levels
    length, width = x_ref.shape
    head_size = width // decay_ref.shape[0]
    lane_groups = width // LANES
    band = width // bands
    band_groups = lane_groups // bands

    def near_place(peer):
        return (peer // 2, 2 * level + peer % 2)

    def far_place(peer):
        return (line, 2 * peer + side)

    def remote(src, dst, send, recv, device):
        return pltpu.make_async_remote_copy(
            src_ref=src, dst_ref=dst, send_sem=send, recv_sem=recv, device_id=device, device_id_type=MESH)

    def region(ref, piece, slot):
        start = pl.multiple_of(piece // shelves * band + slot * cols, cols)
        return ref.at[pl.ds(piece % shelves * rows, rows), pl.ds(start, cols)]

    def go_copy(piece, peer, slot):
        return remote(region(states, piece, peer), arrived.at[piece, slot], go_send.at[piece, peer],
                      go_recv.at[piece, slot], near_place(peer))

    def factor_copy(peer, slot):
        return remote(own_factor.at[peer], factors.at[slot], factor_send.at[peer], factor_recv.at[slot],
                      near_place(peer))

    def up_copy(piece, peer, slot):
        return remote(totals.at[piece, peer], gathered.at[piece, slot], up_send.at[piece, peer],
                      up_recv.at[piece, slot], far_place(peer))

    def span_copy(peer, slot):
        return remote(products, spans.at[slot], span_send.at[peer], span_recv.at[slot], far_place(peer))

    def down_copy(piece, peer, slot):
        return remote(scanned.at[piece, peer], entered.at[piece, slot], down_send.at[piece, peer],
                      down_recv.at[piece, slot], far_place(peer))

    def back_copy(piece, peer, slot):
        return remote(entries.at[piece, peer], region(entry, piece, slot), back_send.at[piece, peer],
                      back_recv.at[piece, slot], near_place(peer))

    barrier = pltpu.get_barrier_semaphore()

    @pl.loop(1, devices)
    def _(step):
        pl.semaphore_signal(
            barrier, inc=1, device_id=place((me + step) % devices), device_id_type=MESH
        )

    proj = halves.at[pl.ds(0, proj_hbm.shape[0])]
    loads = [
        pltpu.make_async_copy(src, dst, load_sem.at[at])
        for at, (src, dst) in enumerate((
            (decay_hbm, decay_ref), (b_hbm, b_ref), (x_hbm, x_ref), (c_hbm, c_ref), (skip_hbm, skip_ref),
            (chosen_hbm, chosen_ref), (gain_hbm, gain_ref), (router_hbm, router_ref), (residual_hbm, residual_ref),
            (proj_hbm, proj), (gate_hbm, gate), (up_hbm, up), (down_hbm, down),
        ))
    ]
    for load in loads[:9]:
        load.start()

    before = (lax.broadcasted_iota(jnp.int32, (length, length), 0) <= lax.broadcasted_iota(
        jnp.int32, (length, length), 1)).astype(jnp.float32)
    loads[0].wait()
    decay_row = decay_ref[...]
    sum_row = jnp.dot(decay_row, before, precision=lax.Precision.HIGHEST, preferred_element_type=jnp.float32)
    weight_row = jnp.sqrt(one_less_exp(2.0 * decay_row))
    sums = sum_row.T
    last = sums[length - 1:length]
    tail_weight = jnp.exp(last - sums) * weight_row.T
    factor = jnp.exp(last)
    for group in range(lane_groups):
        at, start = group * LANES // band, group * LANES % band
        own_factor[start // cols, at, :, start % cols:start % cols + LANES] = per_lane(factor, group, head_size)
    factors[slot_of] = own_factor[slot_of]
    for load in loads[1:6]:
        load.wait()

    for at in range(bands):
        for group in range(at * band_groups, (at + 1) * band_groups):
            columns = slice(group * LANES, (group + 1) * LANES)
            tail_in = x_ref[:, columns].astype(jnp.float32) * per_lane(tail_weight, group, head_size)
            made = lax.dot_general(b_ref[...], tail_in.astype(jnp.bfloat16), (((0,), (0,)), ((), ())),
                                   preferred_element_type=jnp.float32)
            states[:, columns] = made.astype(states.dtype)

        if at == 0:
            pl.semaphore_wait(barrier, devices - 1)

            @pl.loop(1, near, unroll=True)
            def _(step):
                factor_copy((slot_of + step) % near, slot_of).start()

        for piece in range(at * shelves, (at + 1) * shelves):
            @pl.loop(1, near, unroll=True)
            def _(step):
                go_copy(piece, (slot_of + step) % near, slot_of).start()

            arrived[piece, slot_of] = region(states, piece, slot_of)[...]

    loads[9].start()
    scores = lax.dot_general(c_ref[...], b_ref[...], (((1,), (1,)), ((), ())), preferred_element_type=jnp.float32)
    causal = lax.broadcasted_iota(jnp.int32, (length, length), 0) >= lax.broadcasted_iota(
        jnp.int32, (length, length), 1)
    scores = jnp.where(causal, scores, 0.0)

    skip = skip_ref[...]

    def inside(first, stop):
        lane = lax.broadcasted_iota(jnp.int32, (1, LANES), 1)
        count = LANES // head_size
        for group in range(first, stop):
            columns = slice(group * LANES, (group + 1) * LANES)
            x = x_ref[:, columns]
            made = None
            for at in range(count):
                head = group * count + at
                distance = sums[:, head:head + 1] - sum_row[head:head + 1]
                mix = jnp.exp(jnp.minimum(distance, 0.0)) * (weight_row[head:head + 1] * scores)
                one = jnp.dot(mix.astype(jnp.bfloat16), x, preferred_element_type=jnp.float32)
                made = one if at == 0 else jnp.where(lane >= at * head_size, one, made)
            inner[:, columns] = made + per_lane(skip, group, head_size) * x.astype(jnp.float32)

    def sorted_rows():
        chosen = chosen_ref[...]
        choices = hot_ref.shape[0]
        capacity = spread_ref.shape[0] // choices
        hot = (lax.broadcasted_iota(jnp.int32, (choices, length), 0) == chosen).astype(jnp.float32)
        hot_ref[...] = hot
        counts = jnp.dot(hot.astype(jnp.bfloat16), before.astype(jnp.bfloat16), preferred_element_type=jnp.float32)
        slot = jnp.sum(counts * hot, axis=0, keepdims=True).astype(jnp.int32) - 1
        position = chosen * capacity + slot
        spread_ref[...] = (lax.broadcasted_iota(jnp.int32, spread_ref.shape, 0) == position).astype(
            jnp.float32).astype(spread_ref.dtype)

    def pair_totals(piece):
        @pl.loop(1, near, unroll=True)
        def _(step):
            peer = (slot_of + near - step) % near
            if piece == 0:
                factor_copy(peer, peer).wait_recv()
            go_copy(piece, peer, peer).wait_recv()

        if piece == 0:
            @pl.loop(0, lines, unroll=True)
            def _(at):
                products[at] = factors[2 * at] * factors[2 * at + 1]

            spans[level] = products[...]

            @pl.loop(1, levels, unroll=True)
            def _(step):
                span_copy((level + step) % levels, level).start()

        @pl.loop(0, lines, unroll=True)
        def _(at):
            both = factors[2 * at + 1, piece // shelves] * arrived[piece, 2 * at].astype(jnp.float32)
            both = both + arrived[piece, 2 * at + 1].astype(jnp.float32)
            totals[piece, :, at] = both.astype(totals.dtype).reshape(levels, part, cols)

        @pl.loop(1, levels, unroll=True)
        def _(step):
            up_copy(piece, (level + step) % levels, level).start()

        gathered[piece, level] = totals[piece, level]

    def pair_entries(piece):
        @pl.loop(1, levels, unroll=True)
        def _(step):
            peer = (level + levels - step) % levels
            if piece == 0:
                span_copy(peer, peer).wait_recv()
            up_copy(piece, peer, peer).wait_recv()

        def advance(k, state):
            at, floor = k // levels, k % levels
            scanned[piece, floor, at] = state.astype(scanned.dtype)
            return spans[floor, at, piece // shelves] * state + gathered[piece, floor, at].astype(jnp.float32)

        lax.fori_loop(0, lines * levels, advance, jnp.zeros((part, cols), jnp.float32), unroll=True)

        @pl.loop(1, levels, unroll=True)
        def _(step):
            down_copy(piece, (level + step) % levels, level).start()

        entered[piece, level] = scanned[piece, level]

    def block_entries(piece):
        @pl.loop(1, levels, unroll=True)
        def _(step):
            peer = (level + levels - step) % levels
            down_copy(piece, peer, peer).wait_recv()

        @pl.loop(0, lines, unroll=True)
        def _(at):
            first = entered[piece, :, at].reshape(rows, cols)
            entries[piece, 2 * at] = first
            second = factors[2 * at, piece // shelves] * first.astype(jnp.float32)
            second = second + arrived[piece, 2 * at].astype(jnp.float32)
            entries[piece, 2 * at + 1] = second.astype(entries.dtype)

        @pl.loop(1, near, unroll=True)
        def _(step):
            back_copy(piece, (slot_of + step) % near, slot_of).start()

        region(entry, piece, slot_of)[...] = entries[piece, slot_of]

    fill = [lane_groups // 2, 3 * lane_groups // 4, lane_groups]
    inside(0, fill[0])
    for step in range(pieces + 2):
        if step < pieces:
            pair_totals(step)
        if 1 <= step <= pieces:
            pair_entries(step - 1)
        if step >= 2:
            block_entries(step - 2)
        if step < 2:
            inside(fill[step], fill[step + 1])
        if step == 2:
            sorted_rows()

    for load in loads[6:10]:
        load.wait()
    grown = jnp.exp(sums)
    chunk = 512
    squares = jnp.zeros((length, 1), jnp.float32)
    for at in range(bands):
        for piece in range(at * shelves, (at + 1) * shelves):
            @pl.loop(1, near, unroll=True)
            def _(step):
                peer = (slot_of + near - step) % near
                back_copy(piece, peer, peer).wait_recv()

        for group in range(at * band_groups, (at + 1) * band_groups):
            columns = slice(group * LANES, (group + 1) * LANES)
            carried = jnp.dot(c_ref[...], entry[:, columns], preferred_element_type=jnp.float32)
            carried = per_lane(grown, group, head_size) * carried
            scanned_out[:, columns] = (inner[:, columns] + carried).astype(scanned_out.dtype)

        depth = slice(at * band, (at + 1) * band)
        for column in range(0, width, chunk):
            columns = slice(column, column + chunk)
            made = jnp.dot(scanned_out[:, depth], proj[depth, columns], preferred_element_type=jnp.float32)
            if at == 0:
                made = made + residual_ref[:, columns].astype(jnp.float32)
            else:
                made = made + mixed_ref[:, columns]
            mixed_ref[:, columns] = made
            if at == bands - 1:
                squares = squares + jnp.sum(made * made, axis=1, keepdims=True)
    scale = lax.rsqrt(squares / width + 1e-05)
    for column in range(0, width, chunk):
        columns = slice(column, column + chunk)
        normed = (mixed_ref[:, columns] * scale * gain_ref[:, columns]).astype(jnp.bfloat16)
        normed_ref[:, columns] = normed
        made = jnp.dot(spread_ref[...], normed, preferred_element_type=jnp.float32)
        packed_ref[:, :, columns] = made.astype(packed_ref.dtype).reshape(*packed_ref.shape[:2], chunk)
    kernel_ref[...] = jnp.exp(lax.dot_general(
        router_ref[...], normed_ref[...], (((1,), (1,)), ((), ())), preferred_element_type=jnp.float32))

    for load in loads[10:]:
        load.start()
    spots = lax.axis_size("exp")
    mine = me // 2
    experts = devices // 2
    partner = me + 1 - 2 * side
    capacity, width = packed_ref.shape[1:]

    def half(at, slot):
        return halves.at[pl.ds(pl.multiple_of((at * experts + slot) * capacity, capacity), capacity)]
    turns = experts // batch

    def row_copy(other, slot):
        return remote(packed_ref.at[other], rows_ref.at[side, slot], row_send.at[other], row_recv.at[slot],
                      place(2 * other + side))

    def pass_copy(at, slot):
        return remote(rows_ref.at[side, slot], rows_ref.at[at, slot], pass_send.at[slot], pass_recv.at[slot],
                      place(partner))

    def swap_copy(slot):
        return remote(half(1 - side, slot), partial.at[slot], swap_send.at[slot], swap_recv.at[slot],
                      place(partner))

    def home_copy(other, slot):
        return remote(half(side, other), out_ref.at[slot], home_send.at[other], home_recv.at[slot],
                      place(2 * other + side))

    def near_copy(other, slot):
        return remote(kernel_ref, table_ref.at[line, slot], near_send.at[other], near_recv.at[slot],
                      (line, other))

    def far_copy(other, slot):
        return remote(table_ref.at[line], table_ref.at[slot], far_send.at[other], far_recv.at[slot],
                      (other, spot))

    own_rows = pltpu.make_async_copy(packed_ref.at[mine], rows_ref.at[side, mine], own_sem.at[0])
    own_table = pltpu.make_async_copy(kernel_ref, table_ref.at[line, spot], own_sem.at[1])
    own_rows.start()
    own_table.start()
    floors = spots // 2
    row, floor = mine // floors, mine % floors

    def target(k):
        return ((row + k % lines) % lines) * floors + (floor + k // lines) % floors

    def source(k):
        return ((row + lines - k % lines) % lines) * floors + (floor + floors - k // lines) % floors

    @pl.loop(1, spots)
    def _(step):
        near_copy((spot + step) % spots, spot).start()

    @pl.loop(1, experts)
    def _(k):
        row_copy(target(k), mine).start()

    own_rows.wait()
    pass_copy(side, mine).start()

    @pl.loop(0, turns + lag + tail)
    def _(turn):
        @pl.when(turn < turns)
        def _():
            @pl.loop(0, batch)
            def _(at):
                k = turn * batch + at

                @pl.when(k > 0)
                def _():
                    row_copy(source(k), source(k)).wait_recv()
                    pass_copy(side, source(k)).start()

        @pl.when(turn == 0)
        def _():
            for load in loads[10:]:
                load.wait()

        @pl.when((turn >= lag) & (turn < turns + lag))
        def _():
            first = (turn - lag) * batch

            @pl.loop(0, batch)
            def _(at):
                pass_copy(1 - side, source(first + at)).wait_recv()

            sources = [source(first + at) for at in range(batch)]
            places = [(k, src, (k * batch + at) * capacity)
                      for k in range(2) for at, src in enumerate(sources)]
            for k, src, start in places:
                block[start:start + capacity] = rows_ref[k, src]
            taken = block[...]
            across = (((1,), (1,)), ((), ()))
            gate_val = lax.dot_general(taken, gate[...], across, preferred_element_type=jnp.float32)
            up_val = lax.dot_general(taken, up[...], across, preferred_element_type=jnp.float32)
            hidden = (gate_val / (1.0 + jnp.exp(-gate_val)) * up_val).astype(jnp.bfloat16)
            piece = 512
            for column in range(0, width, piece):
                made = jnp.dot(hidden, down[:, column:column + piece], preferred_element_type=jnp.float32)
                made = made.astype(halves.dtype)
                for k, src, start in places:
                    half(k, src)[:, column:column + piece] = made[start:start + capacity]

            @pl.loop(0, batch)
            def _(at):
                swap_copy(source(first + at)).start()

        @pl.when(turn >= lag + tail)
        def _():
            @pl.loop(0, batch)
            def _(at):
                k = (turn - lag - tail) * batch + at
                src = source(k)
                swap_copy(src).wait_recv()
                half(side, src)[...] = (
                    half(side, src)[...].astype(jnp.float32) + partial[src].astype(jnp.float32)
                ).astype(halves.dtype)

                @pl.when(k > 0)
                def _():
                    home_copy(src, mine).start()

        @pl.when(turn == turns // 2)
        def _():
            own_table.wait()

            @pl.loop(1, spots)
            def _(step):
                near_copy((spot + step) % spots, (spot + step) % spots).wait_recv()

            @pl.loop(1, lines)
            def _(step):
                far_copy((line + step) % lines, line).start()

    own_out = pltpu.make_async_copy(half(side, mine), out_ref.at[mine], own_sem.at[0])
    own_out.start()

    @pl.loop(1, lines)
    def _(step):
        other = (line + step) % lines
        far_copy(other, other).wait_recv()
        far_copy(other, other).wait_send()

    choices = kernel_ref.shape[0]

    def sweep(_, column):
        def add(at, totals):
            part = table_ref[at]
            row_scale = 1.0 / jnp.sum(part * column[None], axis=1, keepdims=True)
            return totals + jnp.sum(part * row_scale, axis=0)

        totals = lax.fori_loop(0, lines, add, jnp.zeros((choices, length), jnp.float32))
        return 1.0 / jnp.sum(totals, axis=1, keepdims=True)

    column = lax.fori_loop(0, SINK_ITERS, sweep, jnp.ones((choices, 1), jnp.float32))
    weighted = kernel_ref[...] * column
    picked = jnp.sum(jnp.where(hot_ref[...] > 0.0, weighted, 0.0), axis=0, keepdims=True)
    weight = choices * picked / jnp.sum(weighted, axis=0, keepdims=True)
    weight_ref[...] = weight
    same = lax.broadcasted_iota(jnp.int32, (length, length), 0) == lax.broadcasted_iota(
        jnp.int32, (length, length), 1)
    weight_column = jnp.sum(jnp.where(same, weight, 0.0), axis=1, keepdims=True)

    @pl.loop(1, spots)
    def _(step):
        near_copy((spot + step) % spots, spot).wait_send()

    @pl.loop(0, experts)
    def _(step):
        pass_copy(side, step).wait_send()
        swap_copy(step).wait_send()

    @pl.loop(1, experts)
    def _(step):
        other = (mine + step) % experts
        row_copy(other, other).wait_send()
        home_copy(other, other).wait_recv()
        home_copy(other, other).wait_send()

    own_out.wait()
    for column in range(0, width, 512):
        columns = slice(column, column + 512)
        made = lax.dot_general(spread_ref[...], out_ref[:, :, columns].reshape(experts * capacity, 512),
                               (((0,), (0,)), ((), ())), preferred_element_type=jnp.float32)
        layer_ref[:, columns] = (mixed_ref[:, columns] + weight_column * made).astype(layer_ref.dtype)

    @pl.loop(1, near, unroll=True)
    def _(step):
        peer = (slot_of + near - step) % near
        factor_copy(peer, peer).wait_send()
        for piece in range(pieces):
            go_copy(piece, peer, peer).wait_send()
            back_copy(piece, peer, peer).wait_send()

    @pl.loop(1, levels, unroll=True)
    def _(step):
        peer = (level + levels - step) % levels
        span_copy(peer, peer).wait_send()
        for piece in range(pieces):
            up_copy(piece, peer, peer).wait_send()
            down_copy(piece, peer, peer).wait_send()


def layer(x, residual, b, c, decay, skip, gain, router, assignment, proj, gate_half, up_half, down_half):
    devices = device_count()
    lines, spots = lax.axis_size("seq"), lax.axis_size("exp")
    levels, near, experts = spots // 2, 2 * lines, devices // 2
    length, width = x.shape
    state_size = b.shape[1]
    choices = router.shape[1]
    model_width = proj.shape[1]
    hidden_units = down_half.shape[0]
    capacity = max(16, 2 * length // choices)
    bands = max(1, min(2, width // (near * LANES)))
    shelves = max(1, min(1, state_size // (16 * levels)))
    pieces = bands * shelves
    rows, cols = state_size // shelves, width // (near * bands)
    part = rows // levels
    group, lag, tail = 1, 3, 2
    dma = pltpu.SemaphoreType.DMA
    vmem = pl.BlockSpec(memory_space=pltpu.VMEM)

    def half_words(*shape):
        return pltpu.VMEM(shape, jnp.bfloat16)

    def words(*shape):
        return pltpu.VMEM(shape, jnp.float32)

    flat = half_words(pieces, near, rows, cols)
    deep = half_words(pieces, levels, lines, part, cols)
    single = half_words(experts, capacity, model_width)
    weights = half_words(hidden_units, model_width)
    nears, fars, each = dma((pieces, near)), dma((pieces, levels)), dma((experts,))
    heads = decay.shape[1]
    return pl.pallas_call(
        functools.partial(layer_kernel, bands, shelves, group, lag, tail),
        out_shape=(
            jax.ShapeDtypeStruct((length, model_width), jnp.bfloat16),
            jax.ShapeDtypeStruct((1, length), jnp.float32),
        ),
        in_specs=[pl.BlockSpec(memory_space=pl.ANY)] * 13,
        out_specs=(vmem, vmem),
        scratch_shapes=[
            half_words(length, width), half_words(length, model_width), half_words(length, state_size),
            half_words(length, state_size), words(heads, length), words(1, heads), words(1, model_width),
            half_words(choices, model_width), pltpu.VMEM((1, length), jnp.int32),
            single, words(choices, length), words(choices, length), half_words(choices * capacity, length),
            words(length, model_width),
            half_words(state_size, width), half_words(state_size, width), words(length, width),
            half_words(length, width), half_words(length, model_width), words(near, bands, 1, cols),
            flat, deep, deep, deep, deep, flat, words(near, bands, 1, cols),
            words(lines, bands, 1, cols), words(levels, lines, bands, 1, cols),
            single, words(lines, spots, choices, length), half_words(2, experts, capacity, model_width),
            half_words(max(2 * experts * capacity, width), model_width), single, weights, weights, weights,
            half_words(2 * group * capacity, model_width),
            nears, nears, dma((near,)), dma((near,)), fars, fars,
            dma((levels,)), dma((levels,)), fars, fars, nears, nears,
            each, each, each, each, each, each, each, each,
            dma((spots,)), dma((spots,)), dma((lines,)), dma((lines,)), dma((2,)), dma((13,)),
        ],
        compiler_params=pltpu.CompilerParams(
            collective_id=0, has_side_effects=True, vmem_limit_bytes=60 << 20
        ),
        name="layer",
    )(x, residual, b, c, decay.T, skip[None, :], gain[None, :], router.T, assignment.T, proj,
      gate_half.T, up_half.T, down_half)


def hand_over_kernel(layer_ref, weight_ref, layer_out, weight_out):
    layer_out[...] = layer_ref[...]
    weight_out[...] = weight_ref[...]


def hand_over(layer_out, weight):
    vmem = pl.BlockSpec(memory_space=pltpu.VMEM)
    return pl.pallas_call(
        hand_over_kernel,
        out_shape=(
            jax.ShapeDtypeStruct(layer_out.shape, layer_out.dtype),
            jax.ShapeDtypeStruct(weight.shape, weight.dtype),
        ),
        in_specs=[vmem, vmem],
        out_specs=(vmem, vmem),
        name="hand_over",
    )(layer_out, weight)


def per_device(
    residual_in,
    ssm_input,
    ssm_b,
    ssm_c,
    log_decay,
    skip_gain,
    out_proj,
    norm_gain,
    router,
    assignment,
    expert_gate,
    expert_up,
    expert_down,
):
    layer_out, weight_row = layer(
        ssm_input, residual_in, ssm_b, ssm_c, log_decay, skip_gain, norm_gain, router, assignment, out_proj,
        expert_gate[0], expert_up[0], expert_down[0])
    layer_out, weight_row = hand_over(layer_out, weight_row)
    return (layer_out, weight_row[0])


def solution(mesh):
    in_specs = (
        P(("seq", "exp"), None),
        P(("seq", "exp"), None),
        P(("seq", "exp"), None),
        P(("seq", "exp"), None),
        P(("seq", "exp"), None),
        P(),
        P(),
        P(),
        P(),
        P(("seq", "exp"), None),
        P(("seq", "exp"), None, None),
        P(("seq", "exp"), None, None),
        P(("seq", "exp"), None, None),
    )
    out_specs = (P(("seq", "exp"), None), P(("seq", "exp")))
    return jax.shard_map(
        per_device, mesh=mesh, in_specs=in_specs, out_specs=out_specs, check_vma=False
    )
```
